256 devices in a mesh: seq: 32 (over x, y, core), head: 8 (over z).
Axes of the slice: x: 4, y: 4, z: 8, core: 2. Of those that a mesh axis runs over, the one named last changes fastest.
Arguments:
- queries: bfloat16 [1, 8192, 4096], P(None, 'seq', 'head'), may hold values from -6 to 6
- keys: bfloat16 [1, 8192, 4096], P(None, 'seq', 'head'), may hold values from -6 to 6
- values: bfloat16 [1, 8192, 4096], P(None, 'seq', 'head'), may hold values from -6 to 6
- out_weight: bfloat16 [4096, 4096], P('head'), may hold values from -0.09375 to 0.09375
- out_grad: bfloat16 [1, 8192, 4096], P(None, 'seq', 'head'), may hold values from -6 to 6
- block_doc: int32 [1, 32], replicated, may hold values from 0 to 2, never falling along the last dimension, each value on 1 to 24 neighbouring positions
Outputs:
- context: bfloat16 [1, 8192, 4096], P(None, 'seq', 'head')
- query_grad: bfloat16 [1, 8192, 4096], P(None, 'seq', 'head')
- key_grad: bfloat16 [1, 8192, 4096], P(None, 'seq', 'head')
- value_grad: bfloat16 [1, 8192, 4096], P(None, 'seq', 'head')
- weight_grad: bfloat16 [4096, 4096], P('head', 'seq')
The draws below stay inside these ranges and needn't reach their ends.
Inputs may be any that keep to these rules, and one draw needn't show every extreme that they name: `block_doc`: document numbers never fall along a pack, every document holds whole leaf blocks, and one document covers exactly 24 blocks.
All inputs are finite; a program needn't handle non-finite values.
Results may differ from the reference program's by a relative error of at most 0.019.
Values may be sent and summed in bfloat16 or wider, within the bound.
No kernel may reach another device: no remote copies, remote signals or barrier semaphores. Data moves between devices by JAX's collectives and lax.ppermute only.
A program may use at most 128 MiB of HBM per device.

```python
import math
import jax
import jax.numpy as jnp
import numpy as np
from jax import lax

D = 4096
H = 32
DH = 128
LEAF = 256
BATCH = 1
HD = 4096
NBLK = 32
TOKENS = 8192
LEVELS = 5


def drawn_pair(key):
    shape = (BATCH, NBLK, LEAF, H, DH)
    query_all = jnp.clip(jax.random.normal(jax.random.fold_in(key, 21), shape, jnp.float32), -4.0, 4.0)
    key_all = jnp.clip(jax.random.normal(jax.random.fold_in(key, 22), shape, jnp.float32), -4.0, 4.0)
    return (query_all.reshape(BATCH, TOKENS, H * DH), key_all.reshape(BATCH, TOKENS, H * DH))


def draw_queries(key, part):
    return drawn_pair(key)[0].astype(jnp.bfloat16)


def draw_keys(key, part):
    return drawn_pair(key)[1].astype(jnp.bfloat16)


def spiked(values, key, source, target, blocks, factor):
    owner, partner = [(jnp.arange(values.shape[position]) // (values.shape[position] // blocks)).reshape([-1 if axis == position else 1 for axis in range(values.ndim)]) for position in (source, target)]
    chosen = jax.random.permutation(key, blocks)[partner]
    strong = (owner == chosen) | (owner == (partner + blocks // 2) % blocks)
    return jnp.where(strong, factor * values, values)


def block_levels(rng, shape, pieces, low, top_value):
    level = 1.0
    for dim, shards_of in pieces:
        steps = jax.random.uniform(jax.random.fold_in(jax.random.fold_in(rng, 6), dim), (shards_of,), jnp.float32, low / len(pieces), top_value / len(pieces))
        level = level * jnp.repeat(jnp.exp(steps), shape[dim] // shards_of).reshape((-1,) + (1,) * (len(shape) - 1 - dim))
    return level


def profile(count, total, most, skew):
    loads = [(1 << 20) // math.isqrt(grade ** skew) + 1 for grade in range(2, count + 1)]
    surplus, counts = total - most - (count - 1), [1] * (count - 1)
    while surplus > 0:
        candidates = [i for i in range(count - 1) if counts[i] < most]
        pool, budget = sum([loads[i] for i in candidates]), surplus
        for i in candidates:
            more = min(most - counts[i], max(1, budget * loads[i] // pool), surplus)
            counts[i] = counts[i] + more
            surplus = surplus - more
    return np.array([most] + counts)


def ragged_sizes(stream_key, amount, total, bound, lean):
    if amount == 2:
        one = jax.random.randint(stream_key, (), max(1, total - bound), min(bound, total - 1) + 1)
        return jnp.stack([one, total - one])
    lengths = jnp.asarray(profile(amount, total, bound, lean), jnp.int32)
    couples = (amount - 1) // 2
    donor, receiver = lengths[1:1 + 2 * couples:2], lengths[2:2 + 2 * couples:2]
    room = jnp.minimum(donor - 1, bound - receiver)
    passed = jax.random.randint(jax.random.fold_in(stream_key, 1), (couples,), 0, 1 << 20) % (room + 1)
    lengths = lengths.at[1:1 + 2 * couples:2].set(donor - passed).at[2:2 + 2 * couples:2].set(receiver + passed)
    return lengths[jax.random.permutation(jax.random.fold_in(stream_key, 2), amount)]


def bell_draw(rng, shape, spread, most, shards=(), held_as=jnp.bfloat16):
    values = spread * jax.random.normal(rng, shape, jnp.float32)
    if shards:
        values = values * block_levels(rng, shape, shards, -0.22, 0.18)
    return jnp.clip(values, -most, most).astype(held_as)


def heavy_noise(rng, dims, spread, limit, shards, heavy, kind=jnp.bfloat16):
    values = spread * jax.random.normal(rng, dims, jnp.float32)
    if shards:
        values = values * block_levels(rng, dims, shards, -0.22, 0.18)
    return jnp.clip(spiked(values, jax.random.fold_in(rng, 3), *heavy), -limit, limit).astype(kind)


def setup_inputs(seed: int = 0) -> dict:
    streams_of = jax.random.split(jax.random.key(seed), 7)
    queries = draw_queries(jax.random.fold_in(streams_of[6], 71), 0)
    keys = draw_keys(jax.random.fold_in(streams_of[6], 71), 0)
    values = bell_draw(streams_of[2], (BATCH, TOKENS, HD), 1.0, 6.0, ((1, 32), (2, 8)))
    out_weight = bell_draw(streams_of[3], (HD, D), HD ** -0.5, 0.09375, ((0, 8),))
    out_grad = heavy_noise(streams_of[4], (BATCH, TOKENS, D), 1.0, 6.0, ((1, 32), (2, 8)), (1, 2, 32, 2.75))
    block_doc = jax.vmap(lambda own: jnp.searchsorted(jnp.cumsum(ragged_sizes(own, 3, NBLK, 3 * NBLK // 4, 0)), jnp.arange(NBLK), side="right"))(jax.random.split(streams_of[5], BATCH)).reshape((BATCH, NBLK)).astype(jnp.int32)
    return dict(queries=queries, keys=keys, values=values, out_weight=out_weight, out_grad=out_grad, block_doc=block_doc)


def pool_pairs(blocks):
    pack_count, row_count, features = blocks.shape
    paired = blocks.reshape(pack_count, row_count // 2, 2, features).astype(jnp.float32)
    return ((paired[:, :, 0] + paired[:, :, 1]) * 0.5).astype(jnp.bfloat16)

def spread_pairs(gradient):
    pack_count, row_count, features = gradient.shape
    halved = gradient * 0.5
    return jnp.broadcast_to(halved[:, :, None, :], (pack_count, row_count, 2, features)).reshape(pack_count, 2 * row_count, features)

def round_half(array):
    return lax.optimization_barrier(array.astype(jnp.bfloat16)).astype(jnp.float32)

def add_rows(running, addend, row_start):
    current = lax.dynamic_slice_in_dim(running, row_start, addend.shape[1], 1)
    return lax.dynamic_update_slice_in_dim(running, current + addend, row_start, 1)

def reference(queries, keys, values, out_weight, out_grad, block_doc):
    scaling = 1.0 / math.sqrt(DH)
    columns = LEAF * (LEVELS + 1)
    key_levels = [keys]
    value_levels = [values]
    for level_num in range(1, LEVELS):
        key_levels.append(pool_pairs(key_levels[-1]))
        value_levels.append(pool_pairs(value_levels[-1]))
    context_grad_all = jnp.einsum('btk,hk->bth', out_grad.astype(jnp.float32), out_weight.astype(jnp.float32)).astype(jnp.bfloat16)
    weight_parts = [jnp.ones((2 * LEAF,), jnp.float32)]
    for level_num in range(1, LEVELS):
        weight_parts.append(jnp.full((LEAF,), 2.0 ** level_num, jnp.float32))
    col_weight = jnp.concatenate(weight_parts)
    leaf_iota = jnp.arange(LEAF, dtype=jnp.int32)

    def block_step(carry, block_num):
        key_grads, value_grads, weight_sum = carry
        partner = block_num ^ 1
        row_start = (block_num * LEAF).astype(jnp.int32)
        partner_start = (partner * LEAF).astype(jnp.int32)
        query_block = lax.dynamic_slice_in_dim(queries, row_start, LEAF, 1)
        key_parts = [lax.dynamic_slice_in_dim(keys, row_start, LEAF, 1), lax.dynamic_slice_in_dim(keys, partner_start, LEAF, 1)]
        value_parts = [lax.dynamic_slice_in_dim(values, row_start, LEAF, 1), lax.dynamic_slice_in_dim(values, partner_start, LEAF, 1)]
        block_parts = [jnp.full((LEAF,), block_num, jnp.int32), jnp.full((LEAF,), partner, jnp.int32)]
        level_starts = [row_start, partner_start]
        for level_num in range(1, LEVELS):
            sibling = block_num >> level_num ^ 1
            sib_start = (sibling * LEAF).astype(jnp.int32)
            level_starts.append(sib_start)
            key_parts.append(lax.dynamic_slice_in_dim(key_levels[level_num], sib_start, LEAF, 1))
            value_parts.append(lax.dynamic_slice_in_dim(value_levels[level_num], sib_start, LEAF, 1))
            block_parts.append((sibling << level_num) + leaf_iota // (LEAF >> level_num))
        key_cols = jnp.concatenate(key_parts, axis=1).astype(jnp.float32).reshape(BATCH, columns, H, DH)
        value_cols = jnp.concatenate(value_parts, axis=1).astype(jnp.float32).reshape(BATCH, columns, H, DH)
        col_block = jnp.concatenate(block_parts)
        col_doc = jnp.take(block_doc, col_block, axis=1)
        own_doc = lax.dynamic_slice_in_dim(block_doc, block_num, 1, 1)
        allowed = (col_doc == own_doc)[:, None, None, :]
        query_four = query_block.astype(jnp.float32).reshape(BATCH, LEAF, H, DH)
        scores = jnp.einsum('bthd,bchd->bhtc', query_four, key_cols) * scaling
        masked = jnp.where(allowed, scores, -jnp.inf)
        row_max = lax.optimization_barrier(jnp.max(masked, axis=-1, keepdims=True))
        weights = col_weight * jnp.exp(masked - row_max)
        prob_exact = weights / lax.optimization_barrier(jnp.sum(weights, axis=-1, keepdims=True))
        prob = round_half(prob_exact)
        context_four = round_half(jnp.einsum('bhtc,bchd->bthd', prob, value_cols))
        grad_four = lax.dynamic_slice_in_dim(context_grad_all, row_start, LEAF, 1).astype(jnp.float32).reshape(BATCH, LEAF, H, DH)
        row_delta = jnp.einsum('bthd,bthd->bht', grad_four, context_four)[..., None]
        prob_grad = jnp.einsum('bthd,bchd->bhtc', grad_four, value_cols)
        score_grad = round_half(prob_exact * (prob_grad - row_delta))
        query_grad_block = (jnp.einsum('bhtc,bchd->bthd', score_grad, key_cols) * scaling).astype(jnp.bfloat16).reshape(BATCH, LEAF, HD)
        key_col_grad = (jnp.einsum('bhtc,bthd->bchd', score_grad, query_four) * scaling).reshape(BATCH, columns, HD)
        value_col_grad = jnp.einsum('bhtc,bthd->bchd', prob, grad_four).reshape(BATCH, columns, HD)
        key_grads = list(key_grads)
        value_grads = list(value_grads)
        for piece_num in range(LEVELS + 1):
            level_num = max(piece_num - 1, 0)
            key_piece = key_col_grad[:, piece_num * LEAF:(piece_num + 1) * LEAF]
            value_piece = value_col_grad[:, piece_num * LEAF:(piece_num + 1) * LEAF]
            key_grads[level_num] = add_rows(key_grads[level_num], key_piece, level_starts[piece_num])
            value_grads[level_num] = add_rows(value_grads[level_num], value_piece, level_starts[piece_num])
        context_flat = context_four.reshape(BATCH, LEAF, HD)
        grad_block = lax.dynamic_slice_in_dim(out_grad, row_start, LEAF, 1).astype(jnp.float32)
        partial_block = round_half(jnp.einsum('bth,btk->hk', context_flat, grad_block))
        weight_sum = weight_sum + partial_block
        return ((tuple(key_grads), tuple(value_grads), weight_sum), (context_flat.astype(jnp.bfloat16), query_grad_block))
    zero_levels = tuple((jnp.zeros((BATCH, TOKENS >> level_num, HD), jnp.float32) for level_num in range(LEVELS)))
    start_carry = (zero_levels, zero_levels, jnp.zeros((HD, D), jnp.float32))
    carry, stacked = lax.scan(block_step, start_carry, jnp.arange(NBLK, dtype=jnp.int32))
    key_grads, value_grads, weight_sum = carry
    key_grads = list(key_grads)
    value_grads = list(value_grads)
    for level_num in range(LEVELS - 1, 0, -1):
        key_grads[level_num - 1] = key_grads[level_num - 1] + spread_pairs(key_grads[level_num])
        value_grads[level_num - 1] = value_grads[level_num - 1] + spread_pairs(value_grads[level_num])
    context = jnp.transpose(stacked[0], (1, 0, 2, 3)).reshape(BATCH, TOKENS, HD)
    query_grad = jnp.transpose(stacked[1], (1, 0, 2, 3)).reshape(BATCH, TOKENS, HD)
    return (context, query_grad, key_grads[0].astype(jnp.bfloat16), value_grads[0].astype(jnp.bfloat16), weight_sum.astype(jnp.bfloat16))
```

```python
import functools
import math

import jax
import jax.numpy as jnp
from jax import lax
from jax.experimental import pallas as pl
from jax.experimental.pallas import tpu as pltpu
from jax.sharding import PartitionSpec as P

DH = 128
F32 = jnp.float32
BF16 = jnp.bfloat16
HOPS = (1, 2, 6, 8, 24)


def swapped(value, level_num):
    count = lax.axis_size("seq")
    return lax.ppermute(value, "seq", [(i, i ^ HOPS[level_num]) for i in range(count)])


def mm(a, b, dims):
    return lax.dot_general(a, b, (dims, ((), ())), preferred_element_type=F32)


def pool_matrix(rows):
    r = lax.broadcasted_iota(jnp.int32, (rows // 2, rows), 0)
    c = lax.broadcasted_iota(jnp.int32, (rows // 2, rows), 1)
    return jnp.where((c >> 1) == r, 0.5, 0.0).astype(BF16)


def spread_matrix(rows):
    r = lax.broadcasted_iota(jnp.int32, (rows, rows // 2), 0)
    c = lax.broadcasted_iota(jnp.int32, (rows, rows // 2), 1)
    return jnp.where((r >> 1) == c, 0.5, 0.0).astype(BF16)


def pool_into(out_ref, bit, mine, other):
    rows = mine.shape[0]
    half = rows // 2
    mat = pool_matrix(rows)
    low = mm(mat, mine, ((1,), (0,))).astype(BF16)
    high = mm(mat, other, ((1,), (0,))).astype(BF16)
    out_ref[pl.ds(pl.multiple_of(bit * half, half), half), :] = low
    out_ref[pl.ds(pl.multiple_of((1 - bit) * half, half), half), :] = high


def pool_kernel(level_num, place_ref, mine_ref, other_ref, out_ref):
    bit = (place_ref[0] >> level_num) & 1
    pool_into(out_ref, bit, mine_ref[...], other_ref[...])


def pool_first_kernel(place_ref, key_ref, value_ref, other_key_ref, other_value_ref, out_ref):
    core = place_ref[0] & 1

    @pl.when(core == 0)
    def _():
        pool_into(out_ref, core, key_ref[...], other_key_ref[...])

    @pl.when(core == 1)
    def _():
        pool_into(out_ref, core, value_ref[...], other_value_ref[...])


SMEM = pl.BlockSpec(memory_space=pltpu.SMEM)
VMEM = pl.BlockSpec(memory_space=pltpu.VMEM)


def whole_call(kernel, place, args, outs, scratch=(), name=None):
    return pl.pallas_call(
        kernel,
        in_specs=[SMEM] + [VMEM] * len(args),
        out_specs=[VMEM] * len(outs),
        out_shape=[jax.ShapeDtypeStruct(s, d) for s, d in outs],
        scratch_shapes=list(scratch),
        name=name,
    )(place, *args)


def gather_columns(core, dest_k, dest_v, firsts, mine, other):
    rows = firsts[0].shape[0]
    dest_k[0:rows, :] = firsts[0][...]
    dest_k[rows : 2 * rows, :] = firsts[1][...]
    dest_v[0:rows, :] = firsts[2][...]
    dest_v[rows : 2 * rows, :] = firsts[3][...]

    @pl.when(core == 0)
    def _():
        for i in range(len(mine)):
            dest_k[(2 + i) * rows : (3 + i) * rows, :] = mine[i][...]
            dest_v[(2 + i) * rows : (3 + i) * rows, :] = other[i][...]

    @pl.when(core == 1)
    def _():
        for i in range(len(mine)):
            dest_k[(2 + i) * rows : (3 + i) * rows, :] = other[i][...]
            dest_v[(2 + i) * rows : (3 + i) * rows, :] = mine[i][...]


def forward_kernel(scaling, n_up, place_ref, weight_ref, query_ref, *refs):
    firsts, mine, other = refs[:4], refs[4 : 4 + n_up], refs[4 + n_up : 4 + 2 * n_up]
    context_ref, prob_ref, kcol_ref, vcol_ref = refs[4 + 2 * n_up :]
    gather_columns(place_ref[0] & 1, kcol_ref, vcol_ref, firsts, mine, other)
    col_weight = weight_ref[...]
    scores = mm(query_ref[...], kcol_ref[...], ((1,), (1,))) * scaling
    masked = jnp.where(col_weight > 0.0, scores, -jnp.inf)
    row_max = jnp.max(masked, axis=-1, keepdims=True)
    weights = col_weight * jnp.exp(masked - row_max)
    total = jnp.sum(weights, axis=-1, keepdims=True)
    prob = (weights * (1.0 / total)).astype(BF16)
    prob_ref[0] = prob
    context_ref[...] = mm(prob, vcol_ref[...], ((1,), (0,))).astype(BF16)


def backward_kernel(scaling, n_up, place_ref, query_ref, prob_ref, context_ref, grad_ref, *refs):
    kcol_ref, vcol_ref = refs[:2]
    dq_ref, own_k, own_v, sib_k, sib_v, keep_ref, send_ref = refs[2:]
    core = place_ref[0] & 1
    rows = query_ref.shape[0]
    grad = grad_ref[...]
    prob = prob_ref[0]
    delta = jnp.sum(grad.astype(F32) * context_ref[...].astype(F32), axis=-1, keepdims=True)
    prob_grad = mm(grad, vcol_ref[...], ((1,), (1,)))
    score_grad = (prob.astype(F32) * (prob_grad - delta)).astype(BF16)
    dq_ref[...] = (mm(score_grad, kcol_ref[...], ((1,), (0,))) * scaling).astype(BF16)
    dk = mm(score_grad, query_ref[...], ((0,), (0,))) * scaling
    dv = mm(prob, grad, ((0,), (0,)))
    own_k[...] = dk[:rows]
    own_v[...] = dv[:rows]
    sib_k[...] = dk[rows : 2 * rows]
    sib_v[...] = dv[rows : 2 * rows]
    up_k = dk[2 * rows :].reshape(n_up, rows, DH)
    up_v = dv[2 * rows :].reshape(n_up, rows, DH)

    @pl.when(core == 0)
    def _():
        keep_ref[...] = up_k
        send_ref[...] = up_v.astype(BF16)

    @pl.when(core == 1)
    def _():
        keep_ref[...] = up_v
        send_ref[...] = up_k.astype(BF16)


def spread_half(hi_ref, lo_ref, bit):
    rows = hi_ref.shape[0]
    half = rows // 2
    mat = spread_matrix(rows)
    part = pl.ds(pl.multiple_of(bit * half, half), half)
    return mm(mat, hi_ref[part, :], ((1,), (0,))) + mm(mat, lo_ref[part, :], ((1,), (0,)))


def split_held(hi_ref, lo_ref, held):
    hi = held.astype(BF16)
    hi_ref[...] = hi
    lo_ref[...] = (held - hi.astype(F32)).astype(BF16)


def climb_kernel(level_num, place_ref, held_ref, back_ref, keep_ref, recv_ref, send_ref, own_ref, hi_ref, lo_ref):
    bit = (place_ref[0] >> level_num) & 1
    split_held(hi_ref, lo_ref, held_ref[...] + back_ref[...].astype(F32))
    other = spread_half(hi_ref, lo_ref, 1 - bit)
    send_ref[...] = (keep_ref[0] + recv_ref[0].astype(F32) + other).astype(BF16)
    own_ref[...] = spread_half(hi_ref, lo_ref, bit)


def leaf_kernel(
    place_ref, held_ref, back_ref, own_k, own_v, sib_k, sib_v,
    send_k, send_v, total_k, total_v, hi_ref, lo_ref,
):
    core = place_ref[0] & 1
    split_held(hi_ref, lo_ref, held_ref[...] + back_ref[...].astype(F32))
    other = spread_half(hi_ref, lo_ref, 1 - core)
    own = spread_half(hi_ref, lo_ref, core)
    zero = jnp.zeros_like(own)
    is_key = core == 0
    send_k[...] = (sib_k[...] + jnp.where(is_key, other, zero)).astype(BF16)
    send_v[...] = (sib_v[...] + jnp.where(is_key, zero, other)).astype(BF16)
    total_k[...] = own_k[...] + jnp.where(is_key, own, zero)
    total_v[...] = own_v[...] + jnp.where(is_key, zero, own)


def context_grad_kernel(grad_ref, weight_ref, out_ref, acc_ref):
    step = pl.program_id(0)
    part = mm(grad_ref[0], weight_ref[...], ((1,), (1,)))

    @pl.when(step == 0)
    def _():
        acc_ref[...] = part

    @pl.when(step > 0)
    def _():
        acc_ref[...] += part

    @pl.when(step == pl.num_programs(0) - 1)
    def _():
        out_ref[...] = acc_ref[...].astype(BF16)


def weight_term_kernel(grad_ref, context_ref, out_ref):
    out_ref[...] = mm(grad_ref[0], context_ref[...], ((0,), (0,))).astype(BF16)


def context_grad_of(full_grad, out_weight):
    parts, rows, width = full_grad.shape
    features = out_weight.shape[0]
    return pl.pallas_call(
        context_grad_kernel,
        grid=(parts,),
        in_specs=[
            pl.BlockSpec((1, rows, width), lambda z: (z, 0, 0)),
            pl.BlockSpec((features, width), lambda z: (0, z)),
        ],
        out_specs=pl.BlockSpec((rows, features), lambda z: (0, 0)),
        out_shape=jax.ShapeDtypeStruct((rows, features), BF16),
        scratch_shapes=[pltpu.VMEM((rows, features), F32)],
        name="context_grad",
    )(full_grad, out_weight)


def weight_term_of(full_grad, context):
    parts, rows, width = full_grad.shape
    features = context.shape[1]
    return pl.pallas_call(
        weight_term_kernel,
        grid=(parts,),
        in_specs=[
            pl.BlockSpec((1, rows, width), lambda z: (z, 0, 0)),
            pl.BlockSpec((rows, features), lambda z: (0, 0)),
        ],
        out_specs=pl.BlockSpec((width, features), lambda z: (z, 0)),
        out_shape=jax.ShapeDtypeStruct((parts * width, features), BF16),
        name="weight_term",
    )(full_grad, context)


def column_weights(block_doc, my_block, leaf_rows, level_count):
    leaf_iota = jnp.arange(leaf_rows, dtype=jnp.int32)
    block_parts = [
        jnp.full((leaf_rows,), my_block, jnp.int32),
        jnp.full((leaf_rows,), my_block ^ 1, jnp.int32),
    ]
    weight_parts = [jnp.ones((2 * leaf_rows,), F32)]
    for level_num in range(1, level_count):
        group_first = (my_block >> level_num ^ 1) << level_num
        block_parts.append(group_first + leaf_iota // (leaf_rows >> level_num))
        weight_parts.append(jnp.full((leaf_rows,), 2.0**level_num, F32))
    col_block = jnp.concatenate(block_parts)
    col_weight = jnp.concatenate(weight_parts)
    block_ids = jnp.arange(block_doc.shape[1], dtype=jnp.int32)
    col_onehot = (block_ids[:, None] == col_block[None, :]).astype(jnp.int32)
    col_doc = jnp.sum(block_doc[0][:, None] * col_onehot, axis=0)
    own_doc = jnp.sum(block_doc[0] * (block_ids == my_block).astype(jnp.int32))
    return jnp.where(col_doc == own_doc, col_weight, 0.0)[None]


def local(queries, keys, values, out_weight, out_grad, block_doc):
    seq_count = lax.axis_size("seq")
    level_count = seq_count.bit_length() - 1
    n_up = level_count - 1
    my_block = lax.axis_index("seq")
    place = my_block.astype(jnp.int32)[None]
    _, rows, features = queries.shape
    heads = features // DH
    cols = (level_count + 1) * rows
    scaling = 1.0 / math.sqrt(DH)
    queries, keys, values = queries[0], keys[0], values[0]
    tall = (rows, features)

    other_keys = swapped(keys, 0)
    other_values = swapped(values, 0)
    full_grad = lax.all_gather(out_grad[0], "head")
    (chain,) = whole_call(
        pool_first_kernel, place, (keys, values, other_keys, other_values), [(tall, BF16)], name="pool_leaf"
    )
    mine, other = [], []
    for level_num in range(1, level_count):
        got = swapped(chain, level_num)
        mine.append(got)
        other.append(swapped(got, 0))
        if level_num + 1 < level_count:
            (chain,) = whole_call(
                functools.partial(pool_kernel, level_num), place, (chain, got), [(tall, BF16)], name="pool_group"
            )
    col_weight = column_weights(block_doc, my_block, rows, level_count)
    context_grad = context_grad_of(full_grad, out_weight)

    slab = pl.BlockSpec((rows, DH), lambda h: (0, h))
    col_slab = pl.BlockSpec((cols, DH), lambda h: (0, h))
    prob_slab = pl.BlockSpec((1, rows, cols), lambda h: (h, 0, 0))
    up_slab = pl.BlockSpec((n_up, rows, DH), lambda h: (0, 0, h))
    context, prob, kcols, vcols = pl.pallas_call(
        functools.partial(forward_kernel, scaling, n_up),
        grid=(heads,),
        in_specs=[SMEM, pl.BlockSpec((1, cols), lambda h: (0, 0))] + [slab] * (5 + 2 * n_up),
        out_specs=[slab, prob_slab, col_slab, col_slab],
        out_shape=[
            jax.ShapeDtypeStruct(tall, BF16),
            jax.ShapeDtypeStruct((heads, rows, cols), BF16),
            jax.ShapeDtypeStruct((cols, features), BF16),
            jax.ShapeDtypeStruct((cols, features), BF16),
        ],
        name="attention_forward",
    )(place, col_weight, queries, keys, other_keys, values, other_values, *mine, *other)

    weight_term = weight_term_of(full_grad, context)
    weight_grad = lax.psum_scatter(weight_term, "seq", scatter_dimension=0, tiled=True).T

    query_grad, own_k, own_v, sib_k, sib_v, keep, send_up = pl.pallas_call(
        functools.partial(backward_kernel, scaling, n_up),
        grid=(heads,),
        in_specs=[SMEM, slab, prob_slab, slab, slab, col_slab, col_slab],
        out_specs=[slab] * 5 + [up_slab, up_slab],
        out_shape=[jax.ShapeDtypeStruct(tall, BF16)]
        + [jax.ShapeDtypeStruct(tall, F32)] * 4
        + [
            jax.ShapeDtypeStruct((n_up,) + tall, F32),
            jax.ShapeDtypeStruct((n_up,) + tall, BF16),
        ],
        name="attention_backward",
    )(place, queries, prob, context, context_grad, kcols, vcols)

    recv_up = swapped(send_up, 0)
    top = n_up - 1
    back = swapped((keep[top] + recv_up[top].astype(F32)).astype(BF16), level_count - 1)
    held = jnp.zeros(tall, F32)
    halves = [pltpu.VMEM(tall, BF16), pltpu.VMEM(tall, BF16)]
    for level_num in range(level_count - 2, 0, -1):
        level_block = pl.BlockSpec((1,) + tall, functools.partial(lambda at, i: (at, 0, 0), level_num - 1))
        same = pl.BlockSpec(tall, lambda i: (0, 0))
        send, held = pl.pallas_call(
            functools.partial(climb_kernel, level_num),
            grid=(1,),
            in_specs=[SMEM, same, same, level_block, level_block],
            out_specs=[same, same],
            out_shape=[jax.ShapeDtypeStruct(tall, BF16), jax.ShapeDtypeStruct(tall, F32)],
            scratch_shapes=halves,
            name="hand_down",
        )(place, held, back, keep, recv_up)
        back = swapped(send, level_num)
    send_k, send_v, total_k, total_v = whole_call(
        leaf_kernel,
        place,
        (held, back, own_k, own_v, sib_k, sib_v),
        [(tall, BF16), (tall, BF16), (tall, F32), (tall, F32)],
        scratch=halves,
        name="hand_down_leaf",
    )
    key_grad = (total_k + swapped(send_k, 0).astype(F32)).astype(BF16)
    value_grad = (total_v + swapped(send_v, 0).astype(F32)).astype(BF16)
    return context[None], query_grad[None], key_grad[None], value_grad[None], weight_grad


def solution(mesh):
    placed = (
        P(None, "seq", "head"),
        P(None, "seq", "head"),
        P(None, "seq", "head"),
        P("head", None),
        P(None, "seq", "head"),
        P(),
    )
    return jax.shard_map(
        local,
        mesh=mesh,
        in_specs=placed,
        out_specs=(
            P(None, "seq", "head"),
            P(None, "seq", "head"),
            P(None, "seq", "head"),
            P(None, "seq", "head"),
            P("head", "seq"),
        ),
        check_vma=False,
    )
```

```python
import functools
import math

import jax
import jax.numpy as jnp
from jax import lax
from jax.experimental import pallas as pl
from jax.experimental.pallas import tpu as pltpu
from jax.sharding import PartitionSpec as P

DH = 128
F32 = jnp.float32
BF16 = jnp.bfloat16
HOPS = (1, 2, 6, 8, 24)


def swapped(value, level_num):
    count = lax.axis_size("seq")
    return lax.ppermute(value, "seq", [(i, i ^ HOPS[level_num]) for i in range(count)])


def mm(a, b, dims):
    return lax.dot_general(a, b, (dims, ((), ())), preferred_element_type=F32)


def pool_matrix(rows):
    r = lax.broadcasted_iota(jnp.int32, (rows // 2, rows), 0)
    c = lax.broadcasted_iota(jnp.int32, (rows // 2, rows), 1)
    return jnp.where((c >> 1) == r, 0.5, 0.0).astype(BF16)


def spread_matrix(rows):
    r = lax.broadcasted_iota(jnp.int32, (rows, rows // 2), 0)
    c = lax.broadcasted_iota(jnp.int32, (rows, rows // 2), 1)
    return jnp.where((r >> 1) == c, 0.5, 0.0).astype(BF16)


def pool_into(out_ref, bit, mine, other):
    rows = mine.shape[0]
    half = rows // 2
    mat = pool_matrix(rows)
    low = mm(mat, mine, ((1,), (0,))).astype(BF16)
    high = mm(mat, other, ((1,), (0,))).astype(BF16)
    out_ref[pl.ds(pl.multiple_of(bit * half, half), half), :] = low
    out_ref[pl.ds(pl.multiple_of((1 - bit) * half, half), half), :] = high


def pool_kernel(level_num, place_ref, mine_ref, other_ref, out_ref):
    bit = (place_ref[0] >> level_num) & 1
    pool_into(out_ref, bit, mine_ref[...], other_ref[...])


def pool_first_kernel(place_ref, mine_k, mine_v, other_k, other_v, *out_refs):
    core = place_ref[0] & 1

    def pooled(mine_ref, other_ref):
        width = mine_ref.shape[1] // len(out_refs)
        for i, out_ref in enumerate(out_refs):
            part = slice(i * width, (i + 1) * width)
            pool_into(out_ref, core, mine_ref[:, part], other_ref[:, part])

    pl.when(core == 0)(lambda: pooled(mine_k, other_k))
    pl.when(core == 1)(lambda: pooled(mine_v, other_v))


SMEM = pl.BlockSpec(memory_space=pltpu.SMEM)
VMEM = pl.BlockSpec(memory_space=pltpu.VMEM)


def near_call(kernel, place, args, outs, scratch=(), name=None):
    return pl.pallas_call(
        kernel,
        in_specs=[SMEM] + [VMEM] * len(args),
        out_specs=[VMEM] * len(outs),
        out_shape=[pltpu.VMEM(s, d) for s, d in outs],
        scratch_shapes=list(scratch),
        name=name,
    )(place, *[pltpu.with_memory_space_constraint(a, pltpu.VMEM) for a in args])


def gather_columns(core, dest_k, dest_v, firsts, mine, other):
    rows = firsts[0].shape[0]
    dest_k[0:rows, :] = firsts[0][...]
    dest_k[rows : 2 * rows, :] = firsts[1][...]
    dest_v[0:rows, :] = firsts[2][...]
    dest_v[rows : 2 * rows, :] = firsts[3][...]

    @pl.when(core == 0)
    def _():
        for i in range(len(mine)):
            dest_k[(2 + i) * rows : (3 + i) * rows, :] = mine[i][...]
            dest_v[(2 + i) * rows : (3 + i) * rows, :] = other[i][...]

    @pl.when(core == 1)
    def _():
        for i in range(len(mine)):
            dest_k[(2 + i) * rows : (3 + i) * rows, :] = other[i][...]
            dest_v[(2 + i) * rows : (3 + i) * rows, :] = mine[i][...]


def forward_kernel(scaling, n_up, place_ref, weight_ref, query_ref, *refs):
    firsts, mine, other = refs[:4], refs[4 : 4 + n_up], refs[4 + n_up : 4 + 2 * n_up]
    context_ref, prob_ref, kcol_ref, vcol_ref = refs[4 + 2 * n_up :]
    gather_columns(place_ref[0] & 1, kcol_ref, vcol_ref, firsts, mine, other)
    col_weight = weight_ref[...]
    scores = mm(query_ref[...], kcol_ref[...], ((1,), (1,))) * scaling
    masked = jnp.where(col_weight > 0.0, scores, -jnp.inf)
    row_max = jnp.max(masked, axis=-1, keepdims=True)
    weights = col_weight * jnp.exp(masked - row_max)
    total = jnp.sum(weights, axis=-1, keepdims=True)
    prob = (weights * (1.0 / total)).astype(BF16)
    prob_ref[0] = prob
    context_ref[...] = mm(prob, vcol_ref[...], ((1,), (0,))).astype(BF16)


def backward_kernel(scaling, n_up, place_ref, query_ref, prob_ref, context_ref, grad_ref, *refs):
    kcol_ref, vcol_ref = refs[:2]
    dq_ref, own_k, own_v, sib_k, sib_v, keep_ref, send_ref = refs[2:]
    core = place_ref[0] & 1
    rows = query_ref.shape[0]
    grad = grad_ref[...]
    prob = prob_ref[0]
    delta = jnp.sum(grad.astype(F32) * context_ref[...].astype(F32), axis=-1, keepdims=True)
    prob_grad = mm(grad, vcol_ref[...], ((1,), (1,)))
    score_grad = (prob.astype(F32) * (prob_grad - delta)).astype(BF16)
    dq_ref[...] = (mm(score_grad, kcol_ref[...], ((1,), (0,))) * scaling).astype(BF16)
    dk = mm(score_grad, query_ref[...], ((0,), (0,))) * scaling
    dv = mm(prob, grad, ((0,), (0,)))
    own_k[...] = dk[:rows]
    own_v[...] = dv[:rows]
    sib_k[...] = dk[rows : 2 * rows]
    sib_v[...] = dv[rows : 2 * rows]
    up_k = dk[2 * rows :].reshape(n_up, rows, DH)
    up_v = dv[2 * rows :].reshape(n_up, rows, DH)

    @pl.when(core == 0)
    def _():
        keep_ref[...] = up_k
        send_ref[...] = up_v.astype(BF16)

    @pl.when(core == 1)
    def _():
        keep_ref[...] = up_v
        send_ref[...] = up_k.astype(BF16)


def spread_half(hi_ref, lo_ref, bit):
    rows = hi_ref.shape[0]
    half = rows // 2
    mat = spread_matrix(rows)
    part = pl.ds(pl.multiple_of(bit * half, half), half)
    return mm(mat, hi_ref[part, :], ((1,), (0,))) + mm(mat, lo_ref[part, :], ((1,), (0,)))


def split_held(hi_ref, lo_ref, held):
    hi = held.astype(BF16)
    hi_ref[...] = hi
    lo_ref[...] = (held - hi.astype(F32)).astype(BF16)


def top_kernel(at, place_ref, keep_ref, recv_ref, send_ref):
    send_ref[...] = (keep_ref[at] + recv_ref[at].astype(F32)).astype(BF16)


def climb_kernel(level_num, place_ref, keep_ref, recv_ref, back_ref, *refs):
    held_ref = refs[0] if len(refs) == 5 else None
    send_ref, own_ref, hi_ref, lo_ref = refs[-4:]
    bit = (place_ref[0] >> level_num) & 1
    held = back_ref[...].astype(F32)
    if held_ref is not None:
        held = held + held_ref[...]
    split_held(hi_ref, lo_ref, held)
    other = spread_half(hi_ref, lo_ref, 1 - bit)
    send_ref[...] = (keep_ref[level_num - 1] + recv_ref[level_num - 1].astype(F32) + other).astype(BF16)
    own_ref[...] = spread_half(hi_ref, lo_ref, bit)


def leaf_kernel(
    place_ref, held_ref, back_ref, own_k, own_v, sib_k, sib_v,
    send_k, send_v, total_k, total_v, hi_ref, lo_ref,
):
    core = place_ref[0] & 1
    split_held(hi_ref, lo_ref, held_ref[...] + back_ref[...].astype(F32))
    other = spread_half(hi_ref, lo_ref, 1 - core)
    own = spread_half(hi_ref, lo_ref, core)
    zero = jnp.zeros_like(own)
    is_key = core == 0
    send_k[...] = (sib_k[...] + jnp.where(is_key, other, zero)).astype(BF16)
    send_v[...] = (sib_v[...] + jnp.where(is_key, zero, other)).astype(BF16)
    total_k[...] = own_k[...] + jnp.where(is_key, own, zero)
    total_v[...] = own_v[...] + jnp.where(is_key, zero, own)


def context_grad_kernel(offsets, place_ref, weight_ref, *refs):
    count = len(offsets)
    grads, out_ref, send_ref = refs[:count], refs[count], refs[count + 1]
    core = place_ref[0] & 1
    total = None
    for i, offset in enumerate(offsets):
        at = (place_ref[1] + offset) % count
        width = grads[i].shape[1]
        part = mm(grads[i][...], weight_ref[:, pl.ds(pl.multiple_of(at * width, width), width)], ((1,), (1,)))
        total = part if total is None else total + part
        for j in range(2):
            cols = pl.ds(pl.multiple_of((2 * j + 1 - core) * DH, DH), DH)
            send_ref[i, :, j * DH : (j + 1) * DH] = grads[i][:, cols]
    out_ref[...] = total.astype(BF16)


def weight_term_kernel(offsets, n_parts, place_ref, *refs):
    count = len(offsets)
    grads, other_grads = refs[:count], refs[count]
    mine, other = refs[count + 1 : count + 1 + n_parts], refs[count + 1 + n_parts : count + 1 + 2 * n_parts]
    out_ref, turned_ref = refs[-2:]
    core = place_ref[0] & 1
    rows, width = mine[0].shape
    for i in range(n_parts):
        turned_ref[i * width : (i + 1) * width, :rows] = mine[i][...].astype(F32).T.astype(BF16)
        turned_ref[i * width : (i + 1) * width, rows:] = other[i][...].astype(F32).T.astype(BF16)
    for i, offset in enumerate(offsets):
        at = (place_ref[1] + offset) % count
        own = [grads[i][:, pl.ds(pl.multiple_of((2 * j + core) * DH, DH), DH)] for j in range(2)]
        own = jnp.concatenate(own, axis=1)
        term = mm(turned_ref[:, :rows], own, ((1,), (0,))) + mm(turned_ref[:, rows:], other_grads[i], ((1,), (0,)))
        for j in range(2):
            out_ref[2 * at + j] = term[:, j * DH : (j + 1) * DH].astype(BF16)


def column_weights(block_doc, my_block, leaf_rows, level_count):
    leaf_iota = jnp.arange(leaf_rows, dtype=jnp.int32)
    block_parts = [
        jnp.full((leaf_rows,), my_block, jnp.int32),
        jnp.full((leaf_rows,), my_block ^ 1, jnp.int32),
    ]
    weight_parts = [jnp.ones((2 * leaf_rows,), F32)]
    for level_num in range(1, level_count):
        group_first = (my_block >> level_num ^ 1) << level_num
        block_parts.append(group_first + leaf_iota // (leaf_rows >> level_num))
        weight_parts.append(jnp.full((leaf_rows,), 2.0**level_num, F32))
    col_block = jnp.concatenate(block_parts)
    col_weight = jnp.concatenate(weight_parts)
    block_ids = jnp.arange(block_doc.shape[1], dtype=jnp.int32)
    col_onehot = (block_ids[:, None] == col_block[None, :]).astype(jnp.int32)
    col_doc = jnp.sum(block_doc[0][:, None] * col_onehot, axis=0)
    own_doc = jnp.sum(block_doc[0] * (block_ids == my_block).astype(jnp.int32))
    return jnp.where(col_doc == own_doc, col_weight, 0.0)[None]


def ring_gather(block, axis):
    count = lax.axis_size(axis)
    up = [(i, (i + 1) % count) for i in range(count)]
    down = [(i, (i - 1) % count) for i in range(count)]
    blocks = [(0, block)]
    from_below, from_above = block, block
    for step in range(1, count // 2 + 1):
        from_below = lax.ppermute(from_below, axis, up)
        blocks.append((-step % count, from_below))
        if step < count - step:
            from_above = lax.ppermute(from_above, axis, down)
            blocks.append((step, from_above))
    return blocks


N_PARTS = 2


def local(queries, keys, values, out_weight, out_grad, block_doc):
    seq_count = lax.axis_size("seq")
    level_count = seq_count.bit_length() - 1
    n_up = level_count - 1
    my_block = lax.axis_index("seq")
    place = jnp.stack([my_block, lax.axis_index("head")]).astype(jnp.int32)
    _, rows, features = queries.shape
    heads = features // DH
    part_heads = heads // N_PARTS
    part_width = part_heads * DH
    cols = (level_count + 1) * rows
    scaling = 1.0 / math.sqrt(DH)
    queries, keys, values = queries[0], keys[0], values[0]
    tall = (rows, part_width)

    other_keys = swapped(keys, 0)
    other_values = swapped(values, 0)
    blocks = ring_gather(out_grad[0], "head")
    offsets = tuple(o for o, _ in blocks)
    full_grad = [b for _, b in blocks]
    chains = near_call(
        pool_first_kernel, place, (keys, values, other_keys, other_values), [(tall, BF16)] * N_PARTS, name="pool_leaf"
    )
    chains = list(chains)
    mine, other = [[] for _ in chains], [[] for _ in chains]
    for level_num in range(1, level_count):
        for i in range(N_PARTS):
            got = swapped(chains[i], level_num)
            mine[i].append(got)
            other[i].append(swapped(got, 0))
            if level_num + 1 < level_count:
                (chains[i],) = near_call(
                    functools.partial(pool_kernel, level_num), place, (chains[i], got), [(tall, BF16)], name="pool_group"
                )
    col_weight = column_weights(block_doc, my_block, rows, level_count)
    context_grad, send_grad = pl.pallas_call(
        functools.partial(context_grad_kernel, offsets),
        in_specs=[SMEM] + [VMEM] * (1 + len(offsets)),
        out_specs=[VMEM, VMEM],
        out_shape=[
            jax.ShapeDtypeStruct((rows, features), BF16),
            jax.ShapeDtypeStruct((len(offsets), rows, features // 2), BF16),
        ],
        name="context_grad",
    )(place, out_weight, *full_grad)
    other_grad = swapped(send_grad, 0)

    slab = pl.BlockSpec((rows, DH), lambda h: (0, h))
    col_slab = pl.BlockSpec((cols, DH), lambda h: (0, h))
    prob_slab = pl.BlockSpec((1, rows, cols), lambda h: (h, 0, 0))
    up_slab = pl.BlockSpec((n_up, rows, DH), lambda h: (0, 0, h))
    whole_slabs = [
        pl.BlockSpec((rows, DH), functools.partial(lambda first, h: (0, first + h), i * part_heads))
        for i in range(N_PARTS)
    ]
    forward = []
    for i in range(N_PARTS):
        forward.append(
            pl.pallas_call(
                functools.partial(forward_kernel, scaling, n_up),
                grid=(part_heads,),
                in_specs=[SMEM, pl.BlockSpec((1, cols), lambda h: (0, 0))]
                + [whole_slabs[i]] * 5
                + [slab] * (2 * n_up),
                out_specs=[slab, prob_slab, col_slab, col_slab],
                out_shape=[
                    jax.ShapeDtypeStruct(tall, BF16),
                    jax.ShapeDtypeStruct((part_heads, rows, cols), BF16),
                    jax.ShapeDtypeStruct((cols, part_width), BF16),
                    jax.ShapeDtypeStruct((cols, part_width), BF16),
                ],
                name="attention_forward",
            )(place, col_weight, queries, keys, other_keys, values, other_values, *mine[i], *other[i])
        )
    contexts = [f[0] for f in forward]
    other_contexts = [swapped(c, 0) for c in contexts]

    weight_term = pl.pallas_call(
        functools.partial(weight_term_kernel, offsets, N_PARTS),
        in_specs=[SMEM] + [VMEM] * (len(offsets) + 1 + 2 * N_PARTS),
        out_specs=VMEM,
        out_shape=jax.ShapeDtypeStruct((seq_count // 2, features, DH), BF16),
        scratch_shapes=[pltpu.VMEM((features, 2 * rows), BF16)],
        name="weight_term",
    )(place, *full_grad, other_grad, *contexts, *other_contexts)
    weight_grad = scatter_sum(weight_term, seq_count)

    partial_grads = []
    for i in range(N_PARTS):
        context, prob, kcols, vcols = forward[i]
        partial_grads.append(
            pl.pallas_call(
                functools.partial(backward_kernel, scaling, n_up),
                grid=(part_heads,),
                in_specs=[SMEM, whole_slabs[i], prob_slab, slab, whole_slabs[i], col_slab, col_slab],
                out_specs=[slab] * 5 + [up_slab, up_slab],
                out_shape=[jax.ShapeDtypeStruct(tall, BF16)]
                + [jax.ShapeDtypeStruct(tall, F32)] * 4
                + [
                    jax.ShapeDtypeStruct((n_up,) + tall, F32),
                    jax.ShapeDtypeStruct((n_up,) + tall, BF16),
                ],
                name="attention_backward",
            )(place, queries, prob, context, context_grad, kcols, vcols)
        )
    query_grad = jnp.concatenate([g[0] for g in partial_grads], axis=1)
    halves = [pltpu.VMEM(tall, BF16), pltpu.VMEM(tall, BF16)]
    keep = [g[5] for g in partial_grads]
    recv_up = [swapped(g[6], 0) for g in partial_grads]
    back, held = [None] * N_PARTS, [None] * N_PARTS
    for i in range(N_PARTS):
        (send,) = near_call(
            functools.partial(top_kernel, n_up - 1), place, (keep[i], recv_up[i]), [(tall, BF16)], name="hand_down_top"
        )
        back[i] = swapped(send, level_count - 1)
    for level_num in range(level_count - 2, 0, -1):
        for i in range(N_PARTS):
            args = (keep[i], recv_up[i], back[i]) + (() if held[i] is None else (held[i],))
            send, held[i] = near_call(
                functools.partial(climb_kernel, level_num),
                place,
                args,
                [(tall, BF16), (tall, F32)],
                scratch=halves,
                name="hand_down",
            )
            back[i] = swapped(send, level_num)
    key_grads, value_grads = [], []
    for i in range(N_PARTS):
        send_k, send_v, total_k, total_v = near_call(
            leaf_kernel,
            place,
            (held[i], back[i]) + tuple(partial_grads[i][1:5]),
            [(tall, BF16), (tall, BF16), (tall, F32), (tall, F32)],
            scratch=halves,
            name="hand_down_leaf",
        )
        key_grads.append((total_k + swapped(send_k, 0).astype(F32)).astype(BF16))
        value_grads.append((total_v + swapped(send_v, 0).astype(F32)).astype(BF16))
    context = jnp.concatenate(contexts, axis=1)
    key_grad = jnp.concatenate(key_grads, axis=1)
    value_grad = jnp.concatenate(value_grads, axis=1)
    return context[None], query_grad[None], key_grad[None], value_grad[None], weight_grad


def scatter_sum(weight_term, seq_count):
    groups = [list(range(core, seq_count, 2)) for core in range(2)]
    return lax.psum_scatter(weight_term, "seq", scatter_dimension=0, axis_index_groups=groups, tiled=False)


def solution(mesh):
    placed = (
        P(None, "seq", "head"),
        P(None, "seq", "head"),
        P(None, "seq", "head"),
        P("head", None),
        P(None, "seq", "head"),
        P(),
    )
    return jax.shard_map(
        local,
        mesh=mesh,
        in_specs=placed,
        out_specs=(
            P(None, "seq", "head"),
            P(None, "seq", "head"),
            P(None, "seq", "head"),
            P(None, "seq", "head"),
            P("head", "seq"),
        ),
        check_vma=False,
    )
```

```python
import functools
import math

import jax
import jax.numpy as jnp
from jax import lax
from jax.experimental import pallas as pl
from jax.experimental.pallas import tpu as pltpu
from jax.sharding import PartitionSpec as P

DH = 128
F32 = jnp.float32
BF16 = jnp.bfloat16
HOPS = (1, 2, 6, 8, 24)


def swapped(value, level_num):
    count = lax.axis_size("seq")
    return lax.ppermute(value, "seq", [(i, i ^ HOPS[level_num]) for i in range(count)])


def mm(a, b, dims):
    return lax.dot_general(a, b, (dims, ((), ())), preferred_element_type=F32)


def pool_matrix(rows):
    r = lax.broadcasted_iota(jnp.int32, (rows // 2, rows), 0)
    c = lax.broadcasted_iota(jnp.int32, (rows // 2, rows), 1)
    return jnp.where((c >> 1) == r, 0.5, 0.0).astype(BF16)


def spread_matrix(rows):
    r = lax.broadcasted_iota(jnp.int32, (rows, rows // 2), 0)
    c = lax.broadcasted_iota(jnp.int32, (rows, rows // 2), 1)
    return jnp.where((r >> 1) == c, 0.5, 0.0).astype(BF16)


def pool_into(out_ref, bit, mine, other):
    rows = mine.shape[0]
    half = rows // 2
    mat = pool_matrix(rows)
    low = mm(mat, mine, ((1,), (0,))).astype(BF16)
    high = mm(mat, other, ((1,), (0,))).astype(BF16)
    out_ref[pl.ds(pl.multiple_of(bit * half, half), half), :] = low
    out_ref[pl.ds(pl.multiple_of((1 - bit) * half, half), half), :] = high


def pool_kernel(level_num, place_ref, mine_ref, other_ref, out_ref):
    bit = (place_ref[0] >> level_num) & 1
    pool_into(out_ref, bit, mine_ref[...], other_ref[...])


def pool_first_kernel(place_ref, other_k, other_v, mine_k, mine_v, *out_refs):
    core = place_ref[0] & 1

    def pooled(mine_ref, other_ref):
        width = mine_ref.shape[1] // len(out_refs)
        for i, out_ref in enumerate(out_refs):
            part = slice(i * width, (i + 1) * width)
            pool_into(out_ref, core, mine_ref[:, part], other_ref[:, part])

    pl.when(core == 0)(lambda: pooled(mine_k, other_k))
    pl.when(core == 1)(lambda: pooled(mine_v, other_v))


SMEM = pl.BlockSpec(memory_space=pltpu.SMEM)
VMEM = pl.BlockSpec(memory_space=pltpu.VMEM)


def near_call(kernel, place, near, far, outs, scratch=(), name=None):
    return pl.pallas_call(
        kernel,
        in_specs=[SMEM] + [VMEM] * (len(near) + len(far)),
        out_specs=[VMEM] * len(outs),
        out_shape=[pltpu.VMEM(s, d) if is_near else jax.ShapeDtypeStruct(s, d) for s, d, is_near in outs],
        scratch_shapes=list(scratch),
        name=name,
    )(place, *[pltpu.with_memory_space_constraint(a, pltpu.VMEM) for a in near], *far)


def gather_columns(core, dest_k, dest_v, firsts, mine, other):
    rows = firsts[0].shape[0]
    dest_k[0:rows, :] = firsts[0][...]
    dest_k[rows : 2 * rows, :] = firsts[1][...]
    dest_v[0:rows, :] = firsts[2][...]
    dest_v[rows : 2 * rows, :] = firsts[3][...]

    @pl.when(core == 0)
    def _():
        for i in range(len(mine)):
            dest_k[(2 + i) * rows : (3 + i) * rows, :] = mine[i][...]
            dest_v[(2 + i) * rows : (3 + i) * rows, :] = other[i][...]

    @pl.when(core == 1)
    def _():
        for i in range(len(mine)):
            dest_k[(2 + i) * rows : (3 + i) * rows, :] = other[i][...]
            dest_v[(2 + i) * rows : (3 + i) * rows, :] = mine[i][...]


def forward_kernel(scaling, n_up, place_ref, weight_ref, query_ref, *refs):
    firsts, mine, other = refs[:4], refs[4 : 4 + n_up], refs[4 + n_up : 4 + 2 * n_up]
    context_ref, prob_ref, kcol_ref, vcol_ref = refs[4 + 2 * n_up :]
    gather_columns(place_ref[0] & 1, kcol_ref, vcol_ref, firsts, mine, other)
    col_weight = weight_ref[...]
    scores = mm(query_ref[...], kcol_ref[...], ((1,), (1,))) * scaling
    masked = jnp.where(col_weight > 0.0, scores, -jnp.inf)
    row_max = jnp.max(masked, axis=-1, keepdims=True)
    weights = col_weight * jnp.exp(masked - row_max)
    total = jnp.sum(weights, axis=-1, keepdims=True)
    prob = (weights * (1.0 / total)).astype(BF16)
    prob_ref[0] = prob
    context_ref[...] = mm(prob, vcol_ref[...], ((1,), (0,))).astype(BF16)


def backward_kernel(scaling, n_up, place_ref, query_ref, prob_ref, context_ref, grad_ref, *refs):
    kcol_ref, vcol_ref = refs[:2]
    dq_ref, own_k, own_v, sib_k, sib_v, keep_ref, send_ref = refs[2:]
    core = place_ref[0] & 1
    rows = query_ref.shape[0]
    grad = grad_ref[...]
    prob = prob_ref[0]
    delta = jnp.sum(grad.astype(F32) * context_ref[...].astype(F32), axis=-1, keepdims=True)
    prob_grad = mm(grad, vcol_ref[...], ((1,), (1,)))
    score_grad = (prob.astype(F32) * (prob_grad - delta)).astype(BF16)
    dq_ref[...] = (mm(score_grad, kcol_ref[...], ((1,), (0,))) * scaling).astype(BF16)
    dk = mm(score_grad, query_ref[...], ((0,), (0,))) * scaling
    dv = mm(prob, grad, ((0,), (0,)))
    own_k[...] = dk[:rows]
    own_v[...] = dv[:rows]
    sib_k[...] = dk[rows : 2 * rows]
    sib_v[...] = dv[rows : 2 * rows]
    up_k = dk[2 * rows :].reshape(n_up, rows, DH)
    up_v = dv[2 * rows :].reshape(n_up, rows, DH)

    @pl.when(core == 0)
    def _():
        keep_ref[...] = up_k.astype(BF16)
        send_ref[...] = up_v.astype(BF16)

    @pl.when(core == 1)
    def _():
        keep_ref[...] = up_v.astype(BF16)
        send_ref[...] = up_k.astype(BF16)


def spread_half(hi_ref, lo_ref, bit):
    rows = hi_ref.shape[0]
    half = rows // 2
    mat = spread_matrix(rows)
    part = pl.ds(pl.multiple_of(bit * half, half), half)
    return mm(mat, hi_ref[part, :], ((1,), (0,))) + mm(mat, lo_ref[part, :], ((1,), (0,)))


def split_held(hi_ref, lo_ref, held):
    hi = held.astype(BF16)
    hi_ref[...] = hi
    lo_ref[...] = (held - hi.astype(F32)).astype(BF16)


def top_kernel(place_ref, recv_ref, keep_ref, send_ref, rest_ref):
    top = keep_ref.shape[0] - 1
    send_ref[...] = (keep_ref[top].astype(F32) + recv_ref[top].astype(F32)).astype(BF16)
    rest_ref[...] = keep_ref[:top].astype(F32) + recv_ref[:top].astype(F32)


def climb_kernel(level_num, place_ref, back_ref, rest_ref, *refs):
    held_ref = refs[0] if len(refs) == 5 else None
    send_ref, own_ref, hi_ref, lo_ref = refs[-4:]
    bit = (place_ref[0] >> level_num) & 1
    held = back_ref[...].astype(F32)
    if held_ref is not None:
        held = held + held_ref[...]
    split_held(hi_ref, lo_ref, held)
    other = spread_half(hi_ref, lo_ref, 1 - bit)
    send_ref[...] = (rest_ref[0] + other).astype(BF16)
    own_ref[...] = spread_half(hi_ref, lo_ref, bit)


def leaf_kernel(
    place_ref, back_ref, held_ref, own_k, own_v, sib_k, sib_v,
    send_k, send_v, total_k, total_v, hi_ref, lo_ref,
):
    core = place_ref[0] & 1
    split_held(hi_ref, lo_ref, held_ref[...] + back_ref[...].astype(F32))
    other = spread_half(hi_ref, lo_ref, 1 - core)
    own = spread_half(hi_ref, lo_ref, core)
    zero = jnp.zeros_like(own)
    is_key = core == 0
    send_k[...] = (sib_k[...] + jnp.where(is_key, other, zero)).astype(BF16)
    send_v[...] = (sib_v[...] + jnp.where(is_key, zero, other)).astype(BF16)
    total_k[...] = own_k[...] + jnp.where(is_key, own, zero)
    total_v[...] = own_v[...] + jnp.where(is_key, zero, own)


def context_grad_kernel(offsets, place_ref, depth_ref, weight_ref, *refs):
    count = len(offsets)
    grads, out_ref, send_ref = refs[:count], refs[count], refs[count + 1]
    core = place_ref[0] & 1
    total = None
    for i, offset in enumerate(offsets):
        at = (depth_ref[0] + offset) % count
        width = grads[i].shape[1]
        part = mm(grads[i][...], weight_ref[:, pl.ds(pl.multiple_of(at * width, width), width)], ((1,), (1,)))
        total = part if total is None else total + part
        for j in range(2):
            cols = pl.ds(pl.multiple_of((2 * j + 1 - core) * DH, DH), DH)
            send_ref[i, :, j * DH : (j + 1) * DH] = grads[i][:, cols]
    out_ref[...] = total.astype(BF16)


def slot_of(distance):
    return jnp.where(distance == 0, 0, jnp.where(distance == 3, 1, distance + 1))


def weight_term_kernel(offsets, x_first, place_ref, depth_ref, *refs):
    count = len(offsets)
    grads, other_grads, mine, other = refs[:count], refs[count], refs[count + 1], refs[count + 2]
    send_ref, keep_ref, turned_ref, slots_ref = refs[-4:]
    place = place_ref[0]
    core = place & 1
    rows = mine.shape[0]
    turned_ref[:, :rows] = mine[...].astype(F32).T.astype(BF16)
    turned_ref[:, rows:] = other[...].astype(F32).T.astype(BF16)
    for i, offset in enumerate(offsets):
        at = (depth_ref[0] + offset) % count
        own = [grads[i][:, pl.ds(pl.multiple_of((2 * j + core) * DH, DH), DH)] for j in range(2)]
        own = jnp.concatenate(own, axis=1)
        term = mm(turned_ref[:, :rows], own, ((1,), (0,))) + mm(turned_ref[:, rows:], other_grads[i], ((1,), (0,)))
        for j in range(2):
            chip = 2 * at + j
            slot_x = slot_of((chip >> 2) ^ (place >> 3))
            slot_y = slot_of((chip & 3) ^ ((place >> 1) & 3))
            slot = 4 * slot_x + slot_y if x_first else 4 * slot_y + slot_x
            slots_ref[slot] = term[:, j * DH : (j + 1) * DH].astype(BF16)
    keep_ref[...] = slots_ref[:8]
    send_ref[...] = slots_ref[8:]


def column_weights(block_doc, my_block, leaf_rows, level_count):
    leaf_iota = jnp.arange(leaf_rows, dtype=jnp.int32)
    block_parts = [
        jnp.full((leaf_rows,), my_block, jnp.int32),
        jnp.full((leaf_rows,), my_block ^ 1, jnp.int32),
    ]
    weight_parts = [jnp.ones((2 * leaf_rows,), F32)]
    for level_num in range(1, level_count):
        group_first = (my_block >> level_num ^ 1) << level_num
        block_parts.append(group_first + leaf_iota // (leaf_rows >> level_num))
        weight_parts.append(jnp.full((leaf_rows,), 2.0**level_num, F32))
    col_block = jnp.concatenate(block_parts)
    col_weight = jnp.concatenate(weight_parts)
    block_ids = jnp.arange(block_doc.shape[1], dtype=jnp.int32)
    col_onehot = (block_ids[:, None] == col_block[None, :]).astype(jnp.int32)
    col_doc = jnp.sum(block_doc[0][:, None] * col_onehot, axis=0)
    own_doc = jnp.sum(block_doc[0] * (block_ids == my_block).astype(jnp.int32))
    return jnp.where(col_doc == own_doc, col_weight, 0.0)[None]


class RingGather:
    def __init__(self, block, axis):
        self.axis, self.count = axis, lax.axis_size(axis)
        self.below, self.above, self.steps = block, block, 0
        self.blocks = [(0, block)]

    def step(self, after):
        count, self.steps = self.count, self.steps + 1
        self.below, self.above, _ = lax.optimization_barrier((self.below, self.above, after))
        self.below = lax.ppermute(self.below, self.axis, [(i, (i + 1) % count) for i in range(count)])
        self.blocks.append((-self.steps % count, self.below))
        if self.steps < count - self.steps:
            self.above = lax.ppermute(self.above, self.axis, [(i, (i - 1) % count) for i in range(count)])
            self.blocks.append((self.steps, self.above))


N_PARTS = 2


def local(queries, keys, values, out_weight, out_grad, block_doc):
    seq_count = lax.axis_size("seq")
    level_count = seq_count.bit_length() - 1
    n_up = level_count - 1
    my_block = lax.axis_index("seq")
    place = my_block.astype(jnp.int32)[None]
    depth = lax.axis_index("head").astype(jnp.int32)[None]
    _, rows, features = queries.shape
    heads = features // DH
    part_heads = heads // N_PARTS
    part_width = part_heads * DH
    cols = (level_count + 1) * rows
    scaling = 1.0 / math.sqrt(DH)
    queries, keys, values = queries[0], keys[0], values[0]
    tall = (rows, part_width)

    other_keys = swapped(keys, 0)
    other_values = swapped(values, 0)
    ring = RingGather(out_grad[0], "head")
    ring.step(other_values)
    chains = list(
        near_call(
            pool_first_kernel,
            place,
            (other_keys, other_values),
            (keys, values),
            [(tall, BF16, True)] * N_PARTS,
            name="pool_leaf",
        )
    )
    mine, other = [[] for _ in chains], [[] for _ in chains]
    for level_num in range(1, level_count):
        for i in range(N_PARTS):
            got = swapped(chains[i], level_num)
            mine[i].append(got)
            other[i].append(swapped(got, 0))
            if level_num + 1 < level_count:
                (chains[i],) = near_call(
                    functools.partial(pool_kernel, level_num),
                    place,
                    (chains[i], got),
                    (),
                    [(tall, BF16, True)],
                    name="pool_group",
                )
        if level_num + 1 < level_count:
            ring.step(mine[0][-1])
    offsets = tuple(o for o, _ in ring.blocks)
    full_grad = [b for _, b in ring.blocks]
    col_weight = column_weights(block_doc, my_block, rows, level_count)
    context_grad, send_grad = pl.pallas_call(
        functools.partial(context_grad_kernel, offsets),
        in_specs=[SMEM, SMEM] + [VMEM] * (1 + len(offsets)),
        out_specs=[VMEM, VMEM],
        out_shape=[
            jax.ShapeDtypeStruct((rows, features), BF16),
            jax.ShapeDtypeStruct((len(offsets), rows, features // 2), BF16),
        ],
        name="context_grad",
    )(place, depth, out_weight, *full_grad)
    other_grad = swapped(send_grad, 0)

    slab = pl.BlockSpec((rows, DH), lambda h: (0, h))
    col_slab = pl.BlockSpec((cols, DH), lambda h: (0, h))
    prob_slab = pl.BlockSpec((1, rows, cols), lambda h: (h, 0, 0))
    up_slab = pl.BlockSpec((n_up, rows, DH), lambda h: (0, 0, h))
    whole_slabs = [
        pl.BlockSpec((rows, DH), functools.partial(lambda first, h: (0, first + h), i * part_heads))
        for i in range(N_PARTS)
    ]
    forward = []
    for i in range(N_PARTS):
        forward.append(
            pl.pallas_call(
                functools.partial(forward_kernel, scaling, n_up),
                grid=(part_heads,),
                in_specs=[SMEM, pl.BlockSpec((1, cols), lambda h: (0, 0))]
                + [whole_slabs[i]] * 5
                + [slab] * (2 * n_up),
                out_specs=[slab, prob_slab, col_slab, col_slab],
                out_shape=[
                    jax.ShapeDtypeStruct(tall, BF16),
                    jax.ShapeDtypeStruct((part_heads, rows, cols), BF16),
                    jax.ShapeDtypeStruct((cols, part_width), BF16),
                    jax.ShapeDtypeStruct((cols, part_width), BF16),
                ],
                name="attention_forward",
            )(place, col_weight, queries, keys, other_keys, values, other_values, *mine[i], *other[i])
        )
    contexts = [f[0] for f in forward]
    weight_parts = []
    for i in range(N_PARTS):
        shape = (seq_count // 4, part_width, DH)
        send, keep = pl.pallas_call(
            functools.partial(weight_term_kernel, offsets, i == 0),
            in_specs=[SMEM, SMEM] + [VMEM] * (len(offsets) + 3),
            out_specs=[VMEM, VMEM],
            out_shape=[jax.ShapeDtypeStruct(shape, BF16), jax.ShapeDtypeStruct(shape, BF16)],
            scratch_shapes=[
                pltpu.VMEM((part_width, 2 * rows), BF16),
                pltpu.VMEM((seq_count // 2, part_width, DH), BF16),
            ],
            name="weight_term",
        )(place, depth, *full_grad, other_grad, contexts[i], swapped(contexts[i], 0))
        weight_parts.append(HalvedSum(send, keep, (3, 4, 1, 2) if i == 0 else (1, 2, 3, 4)))
    context_grad = after(context_grad, *[w.send for w in weight_parts])
    partial_grads = []
    for i in range(N_PARTS):
        context, prob, kcols, vcols = forward[i]
        partial_grads.append(
            pl.pallas_call(
                functools.partial(backward_kernel, scaling, n_up),
                grid=(part_heads,),
                in_specs=[SMEM, whole_slabs[i], prob_slab, slab, whole_slabs[i], col_slab, col_slab],
                out_specs=[slab] * 5 + [up_slab, up_slab],
                out_shape=[jax.ShapeDtypeStruct(tall, BF16)]
                + [jax.ShapeDtypeStruct(tall, F32)] * 4
                + [
                    jax.ShapeDtypeStruct((n_up,) + tall, BF16),
                    jax.ShapeDtypeStruct((n_up,) + tall, BF16),
                ],
                name="attention_backward",
            )(place, queries, prob, context, context_grad, kcols, vcols)
        )
    query_grad = jnp.concatenate([g[0] for g in partial_grads], axis=1)
    halves = [pltpu.VMEM(tall, BF16), pltpu.VMEM(tall, BF16)]
    keep = [g[5] for g in partial_grads]
    recv_up = [swapped(g[6], 0) for g in partial_grads]
    back, held, rest = [None] * N_PARTS, [None] * N_PARTS, [None] * N_PARTS
    for i in range(N_PARTS):
        send, rest[i] = near_call(
            top_kernel,
            place,
            (recv_up[i],),
            (keep[i],),
            [(tall, BF16, True), ((n_up - 1,) + tall, F32, False)],
            name="hand_down_top",
        )
        back[i] = swapped(send, level_count - 1)
    for level_num in range(level_count - 2, 0, -1):
        for w in weight_parts:
            w.step()
        for i in range(N_PARTS):
            back[i] = after(back[i], weight_parts[i].send)
            level_rest = rest[i][level_num - 1 : level_num]
            send, held[i] = near_call(
                functools.partial(climb_kernel, level_num),
                place,
                (back[i],),
                (level_rest,) + (() if held[i] is None else (held[i],)),
                [(tall, BF16, True), (tall, F32, False)],
                scratch=halves,
                name="hand_down",
            )
            back[i] = swapped(send, level_num)
    for w in weight_parts:
        w.step()
    weight_grad = jnp.concatenate([w.keep for w in weight_parts], axis=0)
    key_grads, value_grads = [], []
    for i in range(N_PARTS):
        send_k, send_v, total_k, total_v = near_call(
            leaf_kernel,
            place,
            (back[i],),
            (held[i],) + tuple(partial_grads[i][1:5]),
            [(tall, BF16, True), (tall, BF16, True), (tall, F32, False), (tall, F32, False)],
            scratch=halves,
            name="hand_down_leaf",
        )
        key_grads.append((total_k + swapped(send_k, 0).astype(F32)).astype(BF16))
        value_grads.append((total_v + swapped(send_v, 0).astype(F32)).astype(BF16))
    context = jnp.concatenate(contexts, axis=1)
    key_grad = jnp.concatenate(key_grads, axis=1)
    value_grad = jnp.concatenate(value_grads, axis=1)
    return context[None], query_grad[None], key_grad[None], value_grad[None], weight_grad


def after(value, *others):
    return lax.optimization_barrier((value,) + others)[0]


class HalvedSum:
    def __init__(self, send, keep, level_nums):
        self.send, self.keep, self.levels = send, keep, list(level_nums)

    def step(self):
        got = swapped(self.send, self.levels.pop(0))
        total = self.keep.astype(F32) + got.astype(F32)
        half = total.shape[0] // 2
        self.keep, self.send = total[:half], total[half:].astype(BF16)
        if not self.levels:
            self.keep = total[0].astype(BF16)


def solution(mesh):
    placed = (
        P(None, "seq", "head"),
        P(None, "seq", "head"),
        P(None, "seq", "head"),
        P("head", None),
        P(None, "seq", "head"),
        P(),
    )
    return jax.shard_map(
        local,
        mesh=mesh,
        in_specs=placed,
        out_specs=(
            P(None, "seq", "head"),
            P(None, "seq", "head"),
            P(None, "seq", "head"),
            P(None, "seq", "head"),
            P("head", "seq"),
        ),
        check_vma=False,
    )
```

```python
import functools
import math

import jax
import jax.numpy as jnp
from jax import lax
from jax.experimental import pallas as pl
from jax.experimental.pallas import tpu as pltpu
from jax.sharding import PartitionSpec as P

DH = 128
F32 = jnp.float32
BF16 = jnp.bfloat16
HOPS = (1, 2, 6, 8, 24)


def swapped(value, level_num):
    count = lax.axis_size("seq")
    return lax.ppermute(value, "seq", [(i, i ^ HOPS[level_num]) for i in range(count)])


def mm(a, b, dims):
    return lax.dot_general(a, b, (dims, ((), ())), preferred_element_type=F32)


def pool_matrix(rows):
    r = lax.broadcasted_iota(jnp.int32, (rows // 2, rows), 0)
    c = lax.broadcasted_iota(jnp.int32, (rows // 2, rows), 1)
    return jnp.where((c >> 1) == r, 0.5, 0.0).astype(BF16)


def spread_matrix(rows):
    r = lax.broadcasted_iota(jnp.int32, (rows, rows // 2), 0)
    c = lax.broadcasted_iota(jnp.int32, (rows, rows // 2), 1)
    return jnp.where((r >> 1) == c, 0.5, 0.0).astype(BF16)


def pool_into(out_ref, bit, mine, other):
    rows = mine.shape[0]
    half = rows // 2
    mat = pool_matrix(rows)
    low = mm(mat, mine, ((1,), (0,))).astype(BF16)
    high = mm(mat, other, ((1,), (0,))).astype(BF16)
    out_ref[pl.ds(pl.multiple_of(bit * half, half), half), :] = low
    out_ref[pl.ds(pl.multiple_of((1 - bit) * half, half), half), :] = high


def pool_kernel(level_num, place_ref, mine_ref, other_ref, out_ref):
    bit = (place_ref[0] >> level_num) & 1
    pool_into(out_ref, bit, mine_ref[...], other_ref[...])


def pool_first_kernel(place_ref, other_k, other_v, mine_k, mine_v, *out_refs):
    core = place_ref[0] & 1

    def pooled(mine_ref, other_ref):
        width = mine_ref.shape[1] // len(out_refs)
        for i, out_ref in enumerate(out_refs):
            part = slice(i * width, (i + 1) * width)
            pool_into(out_ref, core, mine_ref[:, part], other_ref[:, part])

    pl.when(core == 0)(lambda: pooled(mine_k, other_k))
    pl.when(core == 1)(lambda: pooled(mine_v, other_v))


SMEM = pl.BlockSpec(memory_space=pltpu.SMEM)
VMEM = pl.BlockSpec(memory_space=pltpu.VMEM)


def near_call(kernel, place, near, far, outs, scratch=(), name=None):
    return pl.pallas_call(
        kernel,
        in_specs=[SMEM] + [VMEM] * (len(near) + len(far)),
        out_specs=[VMEM] * len(outs),
        out_shape=[pltpu.VMEM(s, d) if is_near else jax.ShapeDtypeStruct(s, d) for s, d, is_near in outs],
        scratch_shapes=list(scratch),
        name=name,
    )(place, *[pltpu.with_memory_space_constraint(a, pltpu.VMEM) for a in near], *far)


def gather_columns(core, dest_k, dest_v, firsts, mine, other):
    rows = firsts[0].shape[0]
    dest_k[0:rows, :] = firsts[0][...]
    dest_k[rows : 2 * rows, :] = firsts[1][...]
    dest_v[0:rows, :] = firsts[2][...]
    dest_v[rows : 2 * rows, :] = firsts[3][...]

    @pl.when(core == 0)
    def _():
        for i in range(len(mine)):
            dest_k[(2 + i) * rows : (3 + i) * rows, :] = mine[i][...]
            dest_v[(2 + i) * rows : (3 + i) * rows, :] = other[i][...]

    @pl.when(core == 1)
    def _():
        for i in range(len(mine)):
            dest_k[(2 + i) * rows : (3 + i) * rows, :] = other[i][...]
            dest_v[(2 + i) * rows : (3 + i) * rows, :] = mine[i][...]


def forward_kernel(scaling, n_up, place_ref, weight_ref, query_ref, *refs):
    firsts, mine, other = refs[:4], refs[4 : 4 + n_up], refs[4 + n_up : 4 + 2 * n_up]
    context_ref, prob_ref, kcol_ref, vcol_ref = refs[4 + 2 * n_up :]
    gather_columns(place_ref[0] & 1, kcol_ref, vcol_ref, firsts, mine, other)
    col_weight = weight_ref[...]
    scores = mm(query_ref[...], kcol_ref[...], ((1,), (1,))) * scaling
    masked = jnp.where(col_weight > 0.0, scores, -jnp.inf)
    row_max = jnp.max(masked, axis=-1, keepdims=True)
    weights = col_weight * jnp.exp(masked - row_max)
    total = jnp.sum(weights, axis=-1, keepdims=True)
    prob = (weights * (1.0 / total)).astype(BF16)
    prob_ref[0] = prob
    context_ref[...] = mm(prob, vcol_ref[...], ((1,), (0,))).astype(BF16)


def backward_kernel(scaling, n_up, place_ref, query_ref, prob_ref, context_ref, grad_ref, *refs):
    kcol_ref, vcol_ref = refs[:2]
    dq_ref, own_k, own_v, sib_k, sib_v, keep_ref, send_ref = refs[2:]
    core = place_ref[0] & 1
    rows = query_ref.shape[0]
    grad = grad_ref[...]
    prob = prob_ref[0]
    delta = jnp.sum(grad.astype(F32) * context_ref[...].astype(F32), axis=-1, keepdims=True)
    prob_grad = mm(grad, vcol_ref[...], ((1,), (1,)))
    score_grad = (prob.astype(F32) * (prob_grad - delta)).astype(BF16)
    dq_ref[...] = (mm(score_grad, kcol_ref[...], ((1,), (0,))) * scaling).astype(BF16)
    dk = mm(score_grad, query_ref[...], ((0,), (0,))) * scaling
    dv = mm(prob, grad, ((0,), (0,)))
    own_k[...] = dk[:rows]
    own_v[...] = dv[:rows]
    sib_k[...] = dk[rows : 2 * rows]
    sib_v[...] = dv[rows : 2 * rows]
    up_k = dk[2 * rows :].reshape(n_up, rows, DH)
    up_v = dv[2 * rows :].reshape(n_up, rows, DH)

    @pl.when(core == 0)
    def _():
        keep_ref[...] = up_k.astype(BF16)
        send_ref[...] = up_v.astype(BF16)

    @pl.when(core == 1)
    def _():
        keep_ref[...] = up_v.astype(BF16)
        send_ref[...] = up_k.astype(BF16)


def spread_half(hi_ref, lo_ref, bit):
    rows = hi_ref.shape[0]
    half = rows // 2
    mat = spread_matrix(rows)
    part = pl.ds(pl.multiple_of(bit * half, half), half)
    return mm(mat, hi_ref[part, :], ((1,), (0,))) + mm(mat, lo_ref[part, :], ((1,), (0,)))


def split_held(hi_ref, lo_ref, held):
    hi = held.astype(BF16)
    hi_ref[...] = hi
    lo_ref[...] = (held - hi.astype(F32)).astype(BF16)


def top_kernel(place_ref, recv_ref, keep_ref, send_ref, *rest_refs):
    top = keep_ref.shape[0] - 1
    send_ref[...] = (keep_ref[top].astype(F32) + recv_ref[top].astype(F32)).astype(BF16)
    for i, rest_ref in enumerate(rest_refs):
        rest_ref[...] = keep_ref[i].astype(F32) + recv_ref[i].astype(F32)


def climb_kernel(level_num, place_ref, back_ref, rest_ref, *refs):
    held_ref = refs[0] if len(refs) == 5 else None
    send_ref, own_ref, hi_ref, lo_ref = refs[-4:]
    bit = (place_ref[0] >> level_num) & 1
    held = back_ref[...].astype(F32)
    if held_ref is not None:
        held = held + held_ref[...]
    split_held(hi_ref, lo_ref, held)
    other = spread_half(hi_ref, lo_ref, 1 - bit)
    send_ref[...] = (rest_ref[...] + other).astype(BF16)
    own_ref[...] = spread_half(hi_ref, lo_ref, bit)


def leaf_kernel(
    place_ref, back_ref, held_ref, own_k, own_v, sib_k, sib_v,
    send_k, send_v, total_k, total_v, hi_ref, lo_ref,
):
    core = place_ref[0] & 1
    split_held(hi_ref, lo_ref, held_ref[...] + back_ref[...].astype(F32))
    other = spread_half(hi_ref, lo_ref, 1 - core)
    own = spread_half(hi_ref, lo_ref, core)
    zero = jnp.zeros_like(own)
    is_key = core == 0
    send_k[...] = (sib_k[...] + jnp.where(is_key, other, zero)).astype(BF16)
    send_v[...] = (sib_v[...] + jnp.where(is_key, zero, other)).astype(BF16)
    total_k[...] = own_k[...] + jnp.where(is_key, own, zero)
    total_v[...] = own_v[...] + jnp.where(is_key, zero, own)


def context_grad_kernel(offsets, place_ref, depth_ref, weight_ref, *refs):
    count = len(offsets)
    grads, out_ref, send_ref, full_ref = refs[:count], refs[count], refs[count + 1], refs[count + 2]
    acc_ref = refs[count + 3]
    core = place_ref[0] & 1
    width = grads[0].shape[1]
    for i, offset in enumerate(offsets):
        full_ref[(depth_ref[0] + offset) % count] = grads[i][...]
    acc_ref[...] = jnp.zeros_like(acc_ref)

    def add(at, carry):
        acc_ref[...] += mm(full_ref[at], weight_ref[:, pl.ds(pl.multiple_of(at * width, width), width)], ((1,), (1,)))
        for j in range(2):
            cols = pl.ds(pl.multiple_of((2 * j + 1 - core) * DH, DH), DH)
            send_ref[at, :, j * DH : (j + 1) * DH] = full_ref[at, :, cols]
        return carry

    lax.fori_loop(0, count, add, 0)
    out_ref[...] = acc_ref[...].astype(BF16)


def slot_of(distance):
    return jnp.where(distance == 0, 0, jnp.where(distance == 3, 1, distance + 1))


def weight_term_kernel(place_ref, full_ref, other_grads, mine, other, *refs):
    outs, turned_ref, slots = refs[:4], refs[4], refs[5:]
    place = place_ref[0]
    core = place & 1
    rows, width = mine.shape
    part = width // 2
    turned_ref[:, :rows] = mine[...].astype(F32).T.astype(BF16)
    turned_ref[:, rows:] = other[...].astype(F32).T.astype(BF16)

    def term_of(at, carry):
        own = [full_ref[at, :, pl.ds(pl.multiple_of((2 * j + core) * DH, DH), DH)] for j in range(2)]
        own = jnp.concatenate(own, axis=1)
        term = mm(turned_ref[:, :rows], own, ((1,), (0,))) + mm(turned_ref[:, rows:], other_grads[at], ((1,), (0,)))
        term = term.astype(BF16)
        for j in range(2):
            chip = 2 * at + j
            slot_x = slot_of((chip >> 2) ^ (place >> 3))
            slot_y = slot_of((chip & 3) ^ ((place >> 1) & 3))
            slots[0][4 * slot_x + slot_y] = term[:part, j * DH : (j + 1) * DH]
            slots[1][4 * slot_y + slot_x] = term[part:, j * DH : (j + 1) * DH]
        return carry

    lax.fori_loop(0, full_ref.shape[0], term_of, 0)
    half = slots[0].shape[0] // 2
    for i in range(2):
        outs[2 * i][...] = slots[i][half:]
        outs[2 * i + 1][...] = slots[i][:half]


def column_weights(block_doc, my_block, leaf_rows, level_count):
    leaf_iota = jnp.arange(leaf_rows, dtype=jnp.int32)
    block_parts = [
        jnp.full((leaf_rows,), my_block, jnp.int32),
        jnp.full((leaf_rows,), my_block ^ 1, jnp.int32),
    ]
    weight_parts = [jnp.ones((2 * leaf_rows,), F32)]
    for level_num in range(1, level_count):
        group_first = (my_block >> level_num ^ 1) << level_num
        block_parts.append(group_first + leaf_iota // (leaf_rows >> level_num))
        weight_parts.append(jnp.full((leaf_rows,), 2.0**level_num, F32))
    col_block = jnp.concatenate(block_parts)
    col_weight = jnp.concatenate(weight_parts)
    block_ids = jnp.arange(block_doc.shape[1], dtype=jnp.int32)
    col_onehot = (block_ids[:, None] == col_block[None, :]).astype(jnp.int32)
    col_doc = jnp.sum(block_doc[0][:, None] * col_onehot, axis=0)
    own_doc = jnp.sum(block_doc[0] * (block_ids == my_block).astype(jnp.int32))
    return jnp.where(col_doc == own_doc, col_weight, 0.0)[None]


class RingGather:
    def __init__(self, block, axis):
        self.axis, self.count = axis, lax.axis_size(axis)
        self.below, self.above, self.steps = block, block, 0
        self.blocks = [(0, block)]

    def step(self, after):
        count, self.steps = self.count, self.steps + 1
        self.below, self.above, _ = lax.optimization_barrier((self.below, self.above, after))
        self.below = lax.ppermute(self.below, self.axis, [(i, (i + 1) % count) for i in range(count)])
        self.blocks.append((-self.steps % count, self.below))
        if self.steps < count - self.steps:
            self.above = lax.ppermute(self.above, self.axis, [(i, (i - 1) % count) for i in range(count)])
            self.blocks.append((self.steps, self.above))


N_PARTS = 1


def local(queries, keys, values, out_weight, out_grad, block_doc):
    seq_count = lax.axis_size("seq")
    level_count = seq_count.bit_length() - 1
    n_up = level_count - 1
    my_block = lax.axis_index("seq")
    place = my_block.astype(jnp.int32)[None]
    depth = lax.axis_index("head").astype(jnp.int32)[None]
    _, rows, features = queries.shape
    heads = features // DH
    part_heads = heads // N_PARTS
    part_width = part_heads * DH
    cols = (level_count + 1) * rows
    scaling = 1.0 / math.sqrt(DH)
    queries, keys, values = queries[0], keys[0], values[0]
    tall = (rows, part_width)

    other_keys = swapped(keys, 0)
    other_values = swapped(values, 0)
    ring = RingGather(out_grad[0], "head")
    ring.step(other_values)
    chains = list(
        near_call(
            pool_first_kernel,
            place,
            (other_keys, other_values),
            (keys, values),
            [(tall, BF16, True)] * N_PARTS,
            name="pool_leaf",
        )
    )
    mine, other = [[] for _ in chains], [[] for _ in chains]
    for level_num in range(1, level_count):
        for i in range(N_PARTS):
            got = swapped(chains[i], level_num)
            mine[i].append(got)
            other[i].append(swapped(got, 0))
            if level_num + 1 < level_count:
                (chains[i],) = near_call(
                    functools.partial(pool_kernel, level_num),
                    place,
                    (chains[i], got),
                    (),
                    [(tall, BF16, True)],
                    name="pool_group",
                )
        if level_num + 1 < level_count:
            ring.step(mine[0][-1])
    offsets = tuple(o for o, _ in ring.blocks)
    full_grad = [b for _, b in ring.blocks]
    col_weight = column_weights(block_doc, my_block, rows, level_count)
    out_weight = after(out_weight, mine[0][-1])
    context_grad, send_grad, stacked_grad = pl.pallas_call(
        functools.partial(context_grad_kernel, offsets),
        in_specs=[SMEM, SMEM] + [VMEM] * (1 + len(offsets)),
        out_specs=[VMEM, VMEM, VMEM],
        out_shape=[
            jax.ShapeDtypeStruct((rows, features), BF16),
            jax.ShapeDtypeStruct((len(offsets), rows, features // 2), BF16),
            jax.ShapeDtypeStruct((len(offsets), rows, features), BF16),
        ],
        scratch_shapes=[pltpu.VMEM((rows, features), F32)],
        name="context_grad",
    )(place, depth, out_weight, *full_grad)
    other_grad = swapped(send_grad, 0)

    slab = pl.BlockSpec((rows, DH), lambda h: (0, h))
    col_slab = pl.BlockSpec((cols, DH), lambda h: (0, h))
    prob_slab = pl.BlockSpec((1, rows, cols), lambda h: (h, 0, 0))
    up_slab = pl.BlockSpec((n_up, rows, DH), lambda h: (0, 0, h))
    whole_slabs = [
        pl.BlockSpec((rows, DH), functools.partial(lambda first, h: (0, first + h), i * part_heads))
        for i in range(N_PARTS)
    ]
    forward = []
    for i in range(N_PARTS):
        forward.append(
            pl.pallas_call(
                functools.partial(forward_kernel, scaling, n_up),
                grid=(part_heads,),
                in_specs=[SMEM, pl.BlockSpec((1, cols), lambda h: (0, 0))]
                + [whole_slabs[i]] * 5
                + [slab] * (2 * n_up),
                out_specs=[slab, prob_slab, col_slab, col_slab],
                out_shape=[
                    jax.ShapeDtypeStruct(tall, BF16),
                    jax.ShapeDtypeStruct((part_heads, rows, cols), BF16),
                    jax.ShapeDtypeStruct((cols, part_width), BF16),
                    jax.ShapeDtypeStruct((cols, part_width), BF16),
                ],
                name="attention_forward",
            )(place, col_weight, queries, keys, other_keys, values, other_values, *mine[i], *other[i])
        )
    contexts = [f[0] for f in forward]
    (context,) = contexts
    shape = (seq_count // 4, features // 2, DH)
    weight_outs = pl.pallas_call(
        weight_term_kernel,
        in_specs=[SMEM] + [VMEM] * 4,
        out_specs=[VMEM] * 4,
        out_shape=[jax.ShapeDtypeStruct(shape, BF16)] * 4,
        scratch_shapes=[pltpu.VMEM((features, 2 * rows), BF16)]
        + [pltpu.VMEM((seq_count // 2, features // 2, DH), BF16)] * 2,
        name="weight_term",
    )(place, stacked_grad, other_grad, context, swapped(context, 0))
    weight_parts = [
        HalvedSum(weight_outs[0], weight_outs[1], (3, 4, 1, 2)),
        HalvedSum(weight_outs[2], weight_outs[3], (1, 2, 3, 4)),
    ]
    context_grad = after(context_grad, *[w.send for w in weight_parts])
    partial_grads = []
    for i in range(N_PARTS):
        context, prob, kcols, vcols = forward[i]
        partial_grads.append(
            pl.pallas_call(
                functools.partial(backward_kernel, scaling, n_up),
                grid=(part_heads,),
                in_specs=[SMEM, whole_slabs[i], prob_slab, slab, whole_slabs[i], col_slab, col_slab],
                out_specs=[slab] * 5 + [up_slab, up_slab],
                out_shape=[jax.ShapeDtypeStruct(tall, BF16)]
                + [jax.ShapeDtypeStruct(tall, F32)] * 4
                + [
                    jax.ShapeDtypeStruct((n_up,) + tall, BF16),
                    jax.ShapeDtypeStruct((n_up,) + tall, BF16),
                ],
                name="attention_backward",
            )(place, queries, prob, context, context_grad, kcols, vcols)
        )
    query_grad = jnp.concatenate([g[0] for g in partial_grads], axis=1)
    halves = [pltpu.VMEM(tall, BF16), pltpu.VMEM(tall, BF16)]
    keep = [g[5] for g in partial_grads]
    recv_up = [swapped(g[6], 0) for g in partial_grads]
    back, held, rest = [None] * N_PARTS, [None] * N_PARTS, [None] * N_PARTS
    for i in range(N_PARTS):
        send, *rest[i] = near_call(
            top_kernel,
            place,
            (recv_up[i],),
            (keep[i],),
            [(tall, BF16, True)] + [(tall, F32, False)] * (n_up - 1),
            name="hand_down_top",
        )
        back[i] = swapped(send, level_count - 1)
    for level_num in range(level_count - 2, 0, -1):
        for w in weight_parts:
            w.step()
        for i in range(N_PARTS):
            back[i] = after(back[i], *[w.send for w in weight_parts])
            send, held[i] = near_call(
                functools.partial(climb_kernel, level_num),
                place,
                (back[i],),
                (rest[i][level_num - 1],) + (() if held[i] is None else (held[i],)),
                [(tall, BF16, True), (tall, F32, False)],
                scratch=halves,
                name="hand_down",
            )
            back[i] = swapped(send, level_num)
    for w in weight_parts:
        w.step()
    weight_grad = jnp.concatenate([w.keep for w in weight_parts], axis=0)
    key_grads, value_grads = [], []
    for i in range(N_PARTS):
        send_k, send_v, total_k, total_v = near_call(
            leaf_kernel,
            place,
            (back[i],),
            (held[i],) + tuple(partial_grads[i][1:5]),
            [(tall, BF16, True), (tall, BF16, True), (tall, F32, False), (tall, F32, False)],
            scratch=halves,
            name="hand_down_leaf",
        )
        key_grads.append((total_k + swapped(send_k, 0).astype(F32)).astype(BF16))
        value_grads.append((total_v + swapped(send_v, 0).astype(F32)).astype(BF16))
    context = jnp.concatenate(contexts, axis=1)
    key_grad = jnp.concatenate(key_grads, axis=1)
    value_grad = jnp.concatenate(value_grads, axis=1)
    return context[None], query_grad[None], key_grad[None], value_grad[None], weight_grad


def after(value, *others):
    return lax.optimization_barrier((value,) + others)[0]


class HalvedSum:
    def __init__(self, send, keep, level_nums):
        self.send, self.keep, self.levels = send, keep, list(level_nums)

    def step(self):
        got = swapped(self.send, self.levels.pop(0))
        half = self.keep.shape[0] // 2
        if not self.levels:
            self.keep = (self.keep[0].astype(F32) + got[0].astype(F32)).astype(BF16)
            return
        self.send = (self.keep[half:].astype(F32) + got[half:].astype(F32)).astype(BF16)
        self.keep = self.keep[:half].astype(F32) + got[:half].astype(F32)


def solution(mesh):
    placed = (
        P(None, "seq", "head"),
        P(None, "seq", "head"),
        P(None, "seq", "head"),
        P("head", None),
        P(None, "seq", "head"),
        P(),
    )
    return jax.shard_map(
        local,
        mesh=mesh,
        in_specs=placed,
        out_specs=(
            P(None, "seq", "head"),
            P(None, "seq", "head"),
            P(None, "seq", "head"),
            P(None, "seq", "head"),
            P("head", "seq"),
        ),
        check_vma=False,
    )
```

```python
import functools
import math

import jax
import jax.numpy as jnp
from jax import lax
from jax.experimental import pallas as pl
from jax.experimental.pallas import tpu as pltpu
from jax.sharding import PartitionSpec as P

DH = 128
F32 = jnp.float32
BF16 = jnp.bfloat16
HOPS = (1, 2, 6, 8, 24)


def swapped(value, level_num):
    count = lax.axis_size("seq")
    return lax.ppermute(value, "seq", [(i, i ^ HOPS[level_num]) for i in range(count)])


def mm(a, b, dims):
    return lax.dot_general(a, b, (dims, ((), ())), preferred_element_type=F32)


def pool_matrix(rows):
    r = lax.broadcasted_iota(jnp.int32, (rows // 2, rows), 0)
    c = lax.broadcasted_iota(jnp.int32, (rows // 2, rows), 1)
    return jnp.where((c >> 1) == r, 0.5, 0.0).astype(BF16)


def spread_matrix(rows):
    r = lax.broadcasted_iota(jnp.int32, (rows, rows // 2), 0)
    c = lax.broadcasted_iota(jnp.int32, (rows, rows // 2), 1)
    return jnp.where((r >> 1) == c, 0.5, 0.0).astype(BF16)


def pool_into(out_ref, bit, mine, other):
    rows = mine.shape[0]
    half = rows // 2
    mat = pool_matrix(rows)
    low = mm(mat, mine, ((1,), (0,))).astype(BF16)
    high = mm(mat, other, ((1,), (0,))).astype(BF16)
    out_ref[pl.ds(pl.multiple_of(bit * half, half), half), :] = low
    out_ref[pl.ds(pl.multiple_of((1 - bit) * half, half), half), :] = high


def pool_kernel(level_num, place_ref, mine_ref, other_ref, out_ref):
    bit = (place_ref[0] >> level_num) & 1
    pool_into(out_ref, bit, mine_ref[...], other_ref[...])


def pool_first_kernel(place_ref, other_k, other_v, mine_k, mine_v, *out_refs):
    core = place_ref[0] & 1

    def pooled(mine_ref, other_ref):
        width = mine_ref.shape[1] // len(out_refs)
        for i, out_ref in enumerate(out_refs):
            part = slice(i * width, (i + 1) * width)
            pool_into(out_ref, core, mine_ref[:, part], other_ref[:, part])

    pl.when(core == 0)(lambda: pooled(mine_k, other_k))
    pl.when(core == 1)(lambda: pooled(mine_v, other_v))


SMEM = pl.BlockSpec(memory_space=pltpu.SMEM)
VMEM = pl.BlockSpec(memory_space=pltpu.VMEM)


def near_call(kernel, place, near, far, outs, scratch=(), name=None):
    return pl.pallas_call(
        kernel,
        in_specs=[SMEM] + [VMEM] * (len(near) + len(far)),
        out_specs=[VMEM] * len(outs),
        out_shape=[pltpu.VMEM(s, d) if is_near else jax.ShapeDtypeStruct(s, d) for s, d, is_near in outs],
        scratch_shapes=list(scratch),
        name=name,
    )(place, *[pltpu.with_memory_space_constraint(a, pltpu.VMEM) for a in near], *far)


def gather_columns(core, dest_k, dest_v, firsts, mine, other):
    rows = firsts[0].shape[0]
    dest_k[0:rows, :] = firsts[0][...]
    dest_k[rows : 2 * rows, :] = firsts[1][...]
    dest_v[0:rows, :] = firsts[2][...]
    dest_v[rows : 2 * rows, :] = firsts[3][...]

    @pl.when(core == 0)
    def _():
        for i in range(len(mine)):
            dest_k[(2 + i) * rows : (3 + i) * rows, :] = mine[i][...]
            dest_v[(2 + i) * rows : (3 + i) * rows, :] = other[i][...]

    @pl.when(core == 1)
    def _():
        for i in range(len(mine)):
            dest_k[(2 + i) * rows : (3 + i) * rows, :] = other[i][...]
            dest_v[(2 + i) * rows : (3 + i) * rows, :] = mine[i][...]


def forward_kernel(scaling, n_up, place_ref, weight_ref, query_ref, *refs):
    firsts, mine, other = refs[:4], refs[4 : 4 + n_up], refs[4 + n_up : 4 + 2 * n_up]
    context_ref, prob_ref, kcol_ref, vcol_ref = refs[4 + 2 * n_up :]
    gather_columns(place_ref[0] & 1, kcol_ref, vcol_ref, firsts, mine, other)
    col_weight = weight_ref[...]
    scores = mm(query_ref[...], kcol_ref[...], ((1,), (1,))) * scaling
    masked = jnp.where(col_weight > 0.0, scores, -jnp.inf)
    row_max = jnp.max(masked, axis=-1, keepdims=True)
    weights = col_weight * jnp.exp(masked - row_max)
    total = jnp.sum(weights, axis=-1, keepdims=True)
    prob = (weights * (1.0 / total)).astype(BF16)
    prob_ref[0] = prob
    context_ref[...] = mm(prob, vcol_ref[...], ((1,), (0,))).astype(BF16)


def backward_kernel(scaling, n_up, place_ref, query_ref, prob_ref, context_ref, grad_ref, *refs):
    kcol_ref, vcol_ref = refs[:2]
    dq_ref, own_k, own_v, sib_k, sib_v, keep_ref, send_ref = refs[2:]
    core = place_ref[0] & 1
    rows = query_ref.shape[0]
    grad = grad_ref[...]
    prob = prob_ref[0]
    delta = jnp.sum(grad.astype(F32) * context_ref[...].astype(F32), axis=-1, keepdims=True)
    prob_grad = mm(grad, vcol_ref[...], ((1,), (1,)))
    score_grad = (prob.astype(F32) * (prob_grad - delta)).astype(BF16)
    dq_ref[...] = (mm(score_grad, kcol_ref[...], ((1,), (0,))) * scaling).astype(BF16)
    dk = mm(score_grad, query_ref[...], ((0,), (0,))) * scaling
    dv = mm(prob, grad, ((0,), (0,)))
    own_k[...] = dk[:rows].astype(BF16)
    own_v[...] = dv[:rows].astype(BF16)
    sib_k[...] = dk[rows : 2 * rows].astype(BF16)
    sib_v[...] = dv[rows : 2 * rows].astype(BF16)
    up_k = dk[2 * rows :].reshape(n_up, rows, DH)
    up_v = dv[2 * rows :].reshape(n_up, rows, DH)

    @pl.when(core == 0)
    def _():
        keep_ref[...] = up_k.astype(BF16)
        send_ref[...] = up_v.astype(BF16)

    @pl.when(core == 1)
    def _():
        keep_ref[...] = up_v.astype(BF16)
        send_ref[...] = up_k.astype(BF16)


def spread_half(hi_ref, lo_ref, bit):
    rows = hi_ref.shape[0]
    half = rows // 2
    mat = spread_matrix(rows)
    part = pl.ds(pl.multiple_of(bit * half, half), half)
    return mm(mat, hi_ref[part, :], ((1,), (0,))) + mm(mat, lo_ref[part, :], ((1,), (0,)))


def split_held(hi_ref, lo_ref, held):
    hi = held.astype(BF16)
    hi_ref[...] = hi
    lo_ref[...] = (held - hi.astype(F32)).astype(BF16)


def top_kernel(place_ref, recv_ref, keep_ref, send_ref, *rest_refs):
    top = keep_ref.shape[0] - 1
    send_ref[...] = (keep_ref[top].astype(F32) + recv_ref[top].astype(F32)).astype(BF16)
    for i, rest_ref in enumerate(rest_refs):
        rest_ref[...] = (keep_ref[i].astype(F32) + recv_ref[i].astype(F32)).astype(BF16)


def climb_kernel(level_num, place_ref, back_ref, rest_ref, *refs):
    held_ref = refs[0] if len(refs) == 5 else None
    send_ref, own_ref, hi_ref, lo_ref = refs[-4:]
    bit = (place_ref[0] >> level_num) & 1
    held = back_ref[...].astype(F32)
    if held_ref is not None:
        held = held + held_ref[...]
    split_held(hi_ref, lo_ref, held)
    other = spread_half(hi_ref, lo_ref, 1 - bit)
    send_ref[...] = (rest_ref[...].astype(F32) + other).astype(BF16)
    own_ref[...] = spread_half(hi_ref, lo_ref, bit)


def leaf_kernel(
    place_ref, back_ref, held_ref, own_k, own_v, sib_k, sib_v,
    send_k, send_v, total_k, total_v, hi_ref, lo_ref,
):
    core = place_ref[0] & 1
    split_held(hi_ref, lo_ref, held_ref[...] + back_ref[...].astype(F32))
    other = spread_half(hi_ref, lo_ref, 1 - core)
    own = spread_half(hi_ref, lo_ref, core)
    zero = jnp.zeros_like(own)
    is_key = core == 0
    send_k[...] = (sib_k[...].astype(F32) + jnp.where(is_key, other, zero)).astype(BF16)
    send_v[...] = (sib_v[...].astype(F32) + jnp.where(is_key, zero, other)).astype(BF16)
    total_k[...] = own_k[...].astype(F32) + jnp.where(is_key, own, zero)
    total_v[...] = own_v[...].astype(F32) + jnp.where(is_key, zero, own)


def context_grad_kernel(offsets, place_ref, depth_ref, weight_ref, *refs):
    count = len(offsets)
    grads, out_ref, send_ref, full_ref = refs[:count], refs[count], refs[count + 1], refs[count + 2]
    core = place_ref[0] & 1
    width = grads[0].shape[1]
    total = None
    for i, offset in enumerate(offsets):
        at = (depth_ref[0] + offset) % count
        block = grads[i][...]
        full_ref[at] = block
        for j in range(2):
            cols = pl.ds(pl.multiple_of((2 * j + 1 - core) * DH, DH), DH)
            send_ref[at, :, j * DH : (j + 1) * DH] = grads[i][:, cols]
        part = mm(block, weight_ref[:, pl.ds(pl.multiple_of(at * width, width), width)], ((1,), (1,)))
        total = part if total is None else total + part
    out_ref[...] = total.astype(BF16)


def slot_of(distance):
    return jnp.where(distance == 0, 0, jnp.where(distance == 3, 1, distance + 1))


def weight_term_kernel(place_ref, full_ref, other_grads, mine, other, *refs):
    outs, turned_ref, slots = refs[:4], refs[4], refs[5:]
    place = place_ref[0]
    core = place & 1
    rows, width = mine.shape
    part = width // 2
    turned_ref[:, :rows] = mine[...].astype(F32).T.astype(BF16)
    turned_ref[:, rows:] = other[...].astype(F32).T.astype(BF16)

    def term_of(at, carry):
        own = [full_ref[at, :, pl.ds(pl.multiple_of((2 * j + core) * DH, DH), DH)] for j in range(2)]
        own = jnp.concatenate(own, axis=1)
        term = mm(turned_ref[:, :rows], own, ((1,), (0,))) + mm(turned_ref[:, rows:], other_grads[at], ((1,), (0,)))
        term = term.astype(BF16)
        for j in range(2):
            chip = 2 * at + j
            slot_x = slot_of((chip >> 2) ^ (place >> 3))
            slot_y = slot_of((chip & 3) ^ ((place >> 1) & 3))
            slots[0][4 * slot_x + slot_y] = term[:part, j * DH : (j + 1) * DH]
            slots[1][4 * slot_y + slot_x] = term[part:, j * DH : (j + 1) * DH]
        return carry

    lax.fori_loop(0, full_ref.shape[0], term_of, 0)
    half = slots[0].shape[0] // 2
    for i in range(2):
        outs[2 * i][...] = slots[i][half:]
        outs[2 * i + 1][...] = slots[i][:half]


def column_weights(block_doc, my_block, leaf_rows, level_count):
    leaf_iota = jnp.arange(leaf_rows, dtype=jnp.int32)
    block_parts = [
        jnp.full((leaf_rows,), my_block, jnp.int32),
        jnp.full((leaf_rows,), my_block ^ 1, jnp.int32),
    ]
    weight_parts = [jnp.ones((2 * leaf_rows,), F32)]
    for level_num in range(1, level_count):
        group_first = (my_block >> level_num ^ 1) << level_num
        block_parts.append(group_first + leaf_iota // (leaf_rows >> level_num))
        weight_parts.append(jnp.full((leaf_rows,), 2.0**level_num, F32))
    col_block = jnp.concatenate(block_parts)
    col_weight = jnp.concatenate(weight_parts)
    block_ids = jnp.arange(block_doc.shape[1], dtype=jnp.int32)
    col_onehot = (block_ids[:, None] == col_block[None, :]).astype(jnp.int32)
    col_doc = jnp.sum(block_doc[0][:, None] * col_onehot, axis=0)
    own_doc = jnp.sum(block_doc[0] * (block_ids == my_block).astype(jnp.int32))
    return jnp.where(col_doc == own_doc, col_weight, 0.0)[None]


class RingGather:
    def __init__(self, block, axis):
        self.axis, self.count = axis, lax.axis_size(axis)
        self.below, self.above, self.steps = block, block, 0
        self.blocks = [(0, block)]

    def step(self, after):
        count, self.steps = self.count, self.steps + 1
        self.below, self.above, _ = lax.optimization_barrier((self.below, self.above, after))
        self.below = lax.ppermute(self.below, self.axis, [(i, (i + 1) % count) for i in range(count)])
        self.blocks.append((-self.steps % count, self.below))
        if self.steps < count - self.steps:
            self.above = lax.ppermute(self.above, self.axis, [(i, (i - 1) % count) for i in range(count)])
            self.blocks.append((self.steps, self.above))


N_PARTS = 1


def local(queries, keys, values, out_weight, out_grad, block_doc):
    seq_count = lax.axis_size("seq")
    level_count = seq_count.bit_length() - 1
    n_up = level_count - 1
    my_block = lax.axis_index("seq")
    place = my_block.astype(jnp.int32)[None]
    depth = lax.axis_index("head").astype(jnp.int32)[None]
    _, rows, features = queries.shape
    heads = features // DH
    part_heads = heads // N_PARTS
    part_width = part_heads * DH
    cols = (level_count + 1) * rows
    scaling = 1.0 / math.sqrt(DH)
    queries, keys, values = queries[0], keys[0], values[0]
    tall = (rows, part_width)

    other_keys = swapped(keys, 0)
    other_values = swapped(values, 0)
    ring = RingGather(out_grad[0], "head")
    ring.step(other_values)
    chains = list(
        near_call(
            pool_first_kernel,
            place,
            (other_keys, other_values),
            (keys, values),
            [(tall, BF16, True)] * N_PARTS,
            name="pool_leaf",
        )
    )
    mine, other = [[] for _ in chains], [[] for _ in chains]
    for level_num in range(1, level_count):
        for i in range(N_PARTS):
            got = swapped(chains[i], level_num)
            mine[i].append(got)
            other[i].append(swapped(got, 0))
            if level_num + 1 < level_count:
                (chains[i],) = near_call(
                    functools.partial(pool_kernel, level_num),
                    place,
                    (chains[i], got),
                    (),
                    [(tall, BF16, True)],
                    name="pool_group",
                )
        if level_num + 1 < level_count:
            ring.step(chains[0])
    offsets = tuple(o for o, _ in ring.blocks)
    full_grad = [b for _, b in ring.blocks]
    col_weight = column_weights(block_doc, my_block, rows, level_count)
    out_weight = after(out_weight, mine[0][-1])
    context_grad, send_grad, stacked_grad = pl.pallas_call(
        functools.partial(context_grad_kernel, offsets),
        in_specs=[SMEM, SMEM] + [VMEM] * (1 + len(offsets)),
        out_specs=[VMEM, VMEM, VMEM],
        out_shape=[
            jax.ShapeDtypeStruct((rows, features), BF16),
            jax.ShapeDtypeStruct((len(offsets), rows, features // 2), BF16),
            jax.ShapeDtypeStruct((len(offsets), rows, features), BF16),
        ],
        name="context_grad",
    )(place, depth, out_weight, *full_grad)
    other_grad = swapped(send_grad, 0)

    slab = pl.BlockSpec((rows, DH), lambda h: (0, h))
    col_slab = pl.BlockSpec((cols, DH), lambda h: (0, h))
    prob_slab = pl.BlockSpec((1, rows, cols), lambda h: (h, 0, 0))
    up_slab = pl.BlockSpec((n_up, rows, DH), lambda h: (0, 0, h))
    whole_slabs = [
        pl.BlockSpec((rows, DH), functools.partial(lambda first, h: (0, first + h), i * part_heads))
        for i in range(N_PARTS)
    ]
    forward = []
    for i in range(N_PARTS):
        forward.append(
            pl.pallas_call(
                functools.partial(forward_kernel, scaling, n_up),
                grid=(part_heads,),
                in_specs=[SMEM, pl.BlockSpec((1, cols), lambda h: (0, 0))]
                + [whole_slabs[i]] * 5
                + [slab] * (2 * n_up),
                out_specs=[slab, prob_slab, col_slab, col_slab],
                out_shape=[
                    jax.ShapeDtypeStruct(tall, BF16),
                    jax.ShapeDtypeStruct((part_heads, rows, cols), BF16),
                    jax.ShapeDtypeStruct((cols, part_width), BF16),
                    jax.ShapeDtypeStruct((cols, part_width), BF16),
                ],
                name="attention_forward",
            )(place, col_weight, queries, keys, other_keys, values, other_values, *mine[i], *other[i])
        )
    contexts = [f[0] for f in forward]
    (context,) = contexts
    shape = (seq_count // 4, features // 2, DH)
    weight_outs = pl.pallas_call(
        weight_term_kernel,
        in_specs=[SMEM] + [VMEM] * 4,
        out_specs=[VMEM] * 4,
        out_shape=[jax.ShapeDtypeStruct(shape, BF16)] * 4,
        scratch_shapes=[pltpu.VMEM((features, 2 * rows), BF16)]
        + [pltpu.VMEM((seq_count // 2, features // 2, DH), BF16)] * 2,
        name="weight_term",
    )(place, stacked_grad, other_grad, context, swapped(context, 0))
    weight_parts = [
        HalvedSum(weight_outs[0], weight_outs[1], (3, 4, 1, 2)),
        HalvedSum(weight_outs[2], weight_outs[3], (1, 2, 3, 4)),
    ]
    context_grad = after(context_grad, *[w.send for w in weight_parts])
    partial_grads = []
    for i in range(N_PARTS):
        context, prob, kcols, vcols = forward[i]
        partial_grads.append(
            pl.pallas_call(
                functools.partial(backward_kernel, scaling, n_up),
                grid=(part_heads,),
                in_specs=[SMEM, whole_slabs[i], prob_slab, slab, whole_slabs[i], col_slab, col_slab],
                out_specs=[slab] * 5 + [up_slab, up_slab],
                out_shape=[jax.ShapeDtypeStruct(tall, BF16)]
                + [jax.ShapeDtypeStruct(tall, BF16)] * 4
                + [
                    jax.ShapeDtypeStruct((n_up,) + tall, BF16),
                    jax.ShapeDtypeStruct((n_up,) + tall, BF16),
                ],
                name="attention_backward",
            )(place, queries, prob, context, context_grad, kcols, vcols)
        )
    query_grad = jnp.concatenate([g[0] for g in partial_grads], axis=1)
    halves = [pltpu.VMEM(tall, BF16), pltpu.VMEM(tall, BF16)]
    keep = [g[5] for g in partial_grads]
    recv_up = [swapped(g[6], 0) for g in partial_grads]
    back, held, rest = [None] * N_PARTS, [None] * N_PARTS, [None] * N_PARTS
    for i in range(N_PARTS):
        send, *rest[i] = near_call(
            top_kernel,
            place,
            (recv_up[i],),
            (keep[i],),
            [(tall, BF16, True)] + [(tall, BF16, False)] * (n_up - 1),
            name="hand_down_top",
        )
        back[i] = swapped(send, level_count - 1)
        for w in weight_parts:
            w.keep = after(w.keep, send)
    for level_num in range(level_count - 2, 0, -1):
        if level_num < level_count - 2:
            for w in weight_parts:
                w.step()
        for i in range(N_PARTS):
            if level_num < level_count - 2:
                back[i] = after(back[i], *[w.send for w in weight_parts])
            send, held[i] = near_call(
                functools.partial(climb_kernel, level_num),
                place,
                (back[i],),
                (rest[i][level_num - 1],) + (() if held[i] is None else (held[i],)),
                [(tall, BF16, True), (tall, F32, False)],
                scratch=halves,
                name="hand_down",
            )
            back[i] = swapped(send, level_num)
    for w in weight_parts:
        w.step()
    back[-1] = after(back[-1], *[w.send for w in weight_parts])
    for w in weight_parts:
        w.step()
    weight_grad = jnp.concatenate([w.keep for w in weight_parts], axis=0)
    key_grads, value_grads = [], []
    for i in range(N_PARTS):
        send_k, send_v, total_k, total_v = near_call(
            leaf_kernel,
            place,
            (back[i],),
            (held[i],) + tuple(partial_grads[i][1:5]),
            [(tall, BF16, True), (tall, BF16, True), (tall, F32, True), (tall, F32, True)],
            scratch=halves,
            name="hand_down_leaf",
        )
        key_grads.append((total_k + swapped(send_k, 0).astype(F32)).astype(BF16))
        value_grads.append((total_v + swapped(send_v, 0).astype(F32)).astype(BF16))
    context = jnp.concatenate(contexts, axis=1)
    key_grad = jnp.concatenate(key_grads, axis=1)
    value_grad = jnp.concatenate(value_grads, axis=1)
    return context[None], query_grad[None], key_grad[None], value_grad[None], weight_grad


def after(value, *others):
    return lax.optimization_barrier((value,) + others)[0]


class HalvedSum:
    def __init__(self, send, keep, level_nums):
        self.send, self.keep, self.levels = send, keep, list(level_nums)

    def step(self):
        got = swapped(self.send, self.levels.pop(0))
        half = self.keep.shape[0] // 2
        if not self.levels:
            self.keep = (self.keep[0].astype(F32) + got[0].astype(F32)).astype(BF16)
            return
        self.send = (self.keep[half:].astype(F32) + got[half:].astype(F32)).astype(BF16)
        self.keep = self.keep[:half].astype(F32) + got[:half].astype(F32)


def solution(mesh):
    placed = (
        P(None, "seq", "head"),
        P(None, "seq", "head"),
        P(None, "seq", "head"),
        P("head", None),
        P(None, "seq", "head"),
        P(),
    )
    return jax.shard_map(
        local,
        mesh=mesh,
        in_specs=placed,
        out_specs=(
            P(None, "seq", "head"),
            P(None, "seq", "head"),
            P(None, "seq", "head"),
            P(None, "seq", "head"),
            P("head", "seq"),
        ),
        check_vma=False,
    )
```

```python
import functools
import math

import jax
import jax.numpy as jnp
from jax import lax
from jax.experimental import pallas as pl
from jax.experimental.pallas import tpu as pltpu
from jax.sharding import PartitionSpec as P

DH = 128
F32 = jnp.float32
BF16 = jnp.bfloat16
HOPS = (1, 2, 6, 8, 24)


def swapped(value, level_num):
    count = lax.axis_size("seq")
    return lax.ppermute(value, "seq", [(i, i ^ HOPS[level_num]) for i in range(count)])


def mm(a, b, dims):
    return lax.dot_general(a, b, (dims, ((), ())), preferred_element_type=F32)


def pool_matrix(rows):
    r = lax.broadcasted_iota(jnp.int32, (rows // 2, rows), 0)
    c = lax.broadcasted_iota(jnp.int32, (rows // 2, rows), 1)
    return jnp.where((c >> 1) == r, 0.5, 0.0).astype(BF16)


def spread_matrix(rows):
    r = lax.broadcasted_iota(jnp.int32, (rows, rows // 2), 0)
    c = lax.broadcasted_iota(jnp.int32, (rows, rows // 2), 1)
    return jnp.where((r >> 1) == c, 0.5, 0.0).astype(BF16)


def pool_into(out_ref, bit, mine, other):
    rows = mine.shape[0]
    half = rows // 2
    mat = pool_matrix(rows)
    low = mm(mat, mine, ((1,), (0,))).astype(BF16)
    high = mm(mat, other, ((1,), (0,))).astype(BF16)
    out_ref[pl.ds(pl.multiple_of(bit * half, half), half), :] = low
    out_ref[pl.ds(pl.multiple_of((1 - bit) * half, half), half), :] = high


def pool_kernel(level_num, place_ref, mine_ref, other_ref, out_ref):
    bit = (place_ref[0] >> level_num) & 1
    pool_into(out_ref, bit, mine_ref[...], other_ref[...])


def pool_first_kernel(place_ref, other_k, other_v, mine_k, mine_v, *out_refs):
    core = place_ref[0] & 1

    def pooled(mine_ref, other_ref):
        width = mine_ref.shape[1] // len(out_refs)
        for i, out_ref in enumerate(out_refs):
            part = slice(i * width, (i + 1) * width)
            pool_into(out_ref, core, mine_ref[:, part], other_ref[:, part])

    pl.when(core == 0)(lambda: pooled(mine_k, other_k))
    pl.when(core == 1)(lambda: pooled(mine_v, other_v))


SMEM = pl.BlockSpec(memory_space=pltpu.SMEM)
VMEM = pl.BlockSpec(memory_space=pltpu.VMEM)


def near_call(kernel, place, near, far, outs, scratch=(), name=None):
    return pl.pallas_call(
        kernel,
        in_specs=[SMEM] + [VMEM] * (len(near) + len(far)),
        out_specs=[VMEM] * len(outs),
        out_shape=[pltpu.VMEM(s, d) if is_near else jax.ShapeDtypeStruct(s, d) for s, d, is_near in outs],
        scratch_shapes=list(scratch),
        name=name,
    )(place, *[pltpu.with_memory_space_constraint(a, pltpu.VMEM) for a in near], *far)


def gather_columns(core, dest_k, dest_v, firsts, mine, other):
    rows = firsts[0].shape[0]
    dest_k[0:rows, :] = firsts[0][...]
    dest_k[rows : 2 * rows, :] = firsts[1][...]
    dest_v[0:rows, :] = firsts[2][...]
    dest_v[rows : 2 * rows, :] = firsts[3][...]

    @pl.when(core == 0)
    def _():
        for i in range(len(mine)):
            dest_k[(2 + i) * rows : (3 + i) * rows, :] = mine[i][...]
            dest_v[(2 + i) * rows : (3 + i) * rows, :] = other[i][...]

    @pl.when(core == 1)
    def _():
        for i in range(len(mine)):
            dest_k[(2 + i) * rows : (3 + i) * rows, :] = other[i][...]
            dest_v[(2 + i) * rows : (3 + i) * rows, :] = mine[i][...]


def forward_kernel(scaling, n_up, place_ref, weight_ref, query_ref, *refs):
    firsts, mine, other = refs[:4], refs[4 : 4 + n_up], refs[4 + n_up : 4 + 2 * n_up]
    context_ref, prob_ref, kcol_ref, vcol_ref = refs[4 + 2 * n_up :]
    gather_columns(place_ref[0] & 1, kcol_ref, vcol_ref, firsts, mine, other)
    col_weight = weight_ref[...]
    scores = mm(query_ref[...], kcol_ref[...], ((1,), (1,))) * scaling
    masked = jnp.where(col_weight > 0.0, scores, -jnp.inf)
    row_max = jnp.max(masked, axis=-1, keepdims=True)
    weights = col_weight * jnp.exp(masked - row_max)
    total = jnp.sum(weights, axis=-1, keepdims=True)
    prob = (weights * (1.0 / total)).astype(BF16)
    prob_ref[0] = prob
    context_ref[...] = mm(prob, vcol_ref[...], ((1,), (0,))).astype(BF16)


def backward_kernel(scaling, n_up, place_ref, query_ref, prob_ref, context_ref, grad_ref, *refs):
    kcol_ref, vcol_ref = refs[:2]
    dq_ref, own_k, own_v, sib_k, sib_v, keep_ref, send_ref = refs[2:]
    core = place_ref[0] & 1
    rows = query_ref.shape[0]
    grad = grad_ref[...]
    prob = prob_ref[0]
    delta = jnp.sum(grad.astype(F32) * context_ref[...].astype(F32), axis=-1, keepdims=True)
    prob_grad = mm(grad, vcol_ref[...], ((1,), (1,)))
    score_grad = (prob.astype(F32) * (prob_grad - delta)).astype(BF16)
    dq_ref[...] = (mm(score_grad, kcol_ref[...], ((1,), (0,))) * scaling).astype(BF16)
    dk = mm(score_grad, query_ref[...], ((0,), (0,))) * scaling
    dv = mm(prob, grad, ((0,), (0,)))
    own_k[...] = dk[:rows].astype(BF16)
    own_v[...] = dv[:rows].astype(BF16)
    sib_k[...] = dk[rows : 2 * rows].astype(BF16)
    sib_v[...] = dv[rows : 2 * rows].astype(BF16)
    up_k = dk[2 * rows :].reshape(n_up, rows, DH)
    up_v = dv[2 * rows :].reshape(n_up, rows, DH)

    @pl.when(core == 0)
    def _():
        keep_ref[...] = up_k.astype(BF16)
        send_ref[...] = up_v.astype(BF16)

    @pl.when(core == 1)
    def _():
        keep_ref[...] = up_v.astype(BF16)
        send_ref[...] = up_k.astype(BF16)


def spread_half(hi_ref, lo_ref, bit):
    rows = hi_ref.shape[0]
    half = rows // 2
    mat = spread_matrix(rows)
    part = pl.ds(pl.multiple_of(bit * half, half), half)
    return mm(mat, hi_ref[part, :], ((1,), (0,))) + mm(mat, lo_ref[part, :], ((1,), (0,)))


def split_held(hi_ref, lo_ref, held):
    hi = held.astype(BF16)
    hi_ref[...] = hi
    lo_ref[...] = (held - hi.astype(F32)).astype(BF16)


def top_kernel(place_ref, recv_ref, keep_ref, send_ref, *rest_refs):
    top = keep_ref.shape[0] - 1
    send_ref[...] = (keep_ref[top].astype(F32) + recv_ref[top].astype(F32)).astype(BF16)
    for i, rest_ref in enumerate(rest_refs):
        rest_ref[...] = (keep_ref[i].astype(F32) + recv_ref[i].astype(F32)).astype(BF16)


def climb_kernel(level_num, place_ref, back_ref, rest_ref, *refs):
    held_ref = refs[0] if len(refs) == 5 else None
    send_ref, own_ref, hi_ref, lo_ref = refs[-4:]
    bit = (place_ref[0] >> level_num) & 1
    held = back_ref[...].astype(F32)
    if held_ref is not None:
        held = held + held_ref[...]
    split_held(hi_ref, lo_ref, held)
    other = spread_half(hi_ref, lo_ref, 1 - bit)
    send_ref[...] = (rest_ref[...].astype(F32) + other).astype(BF16)
    own_ref[...] = spread_half(hi_ref, lo_ref, bit)


def leaf_kernel(
    place_ref, back_ref, held_ref, own_k, own_v, sib_k, sib_v,
    send_k, send_v, total_k, total_v, hi_ref, lo_ref,
):
    core = place_ref[0] & 1
    split_held(hi_ref, lo_ref, held_ref[...] + back_ref[...].astype(F32))
    other = spread_half(hi_ref, lo_ref, 1 - core)
    own = spread_half(hi_ref, lo_ref, core)
    zero = jnp.zeros_like(own)
    is_key = core == 0
    send_k[...] = (sib_k[...].astype(F32) + jnp.where(is_key, other, zero)).astype(BF16)
    send_v[...] = (sib_v[...].astype(F32) + jnp.where(is_key, zero, other)).astype(BF16)
    total_k[...] = own_k[...].astype(F32) + jnp.where(is_key, own, zero)
    total_v[...] = own_v[...].astype(F32) + jnp.where(is_key, zero, own)


def context_grad_kernel(offsets, place_ref, depth_ref, weight_ref, *refs):
    count = len(offsets)
    grads, out_ref, send_ref, full_ref = refs[:count], refs[count], refs[count + 1], refs[count + 2]
    core = place_ref[0] & 1
    width = grads[0].shape[1]
    total = None
    for i, offset in enumerate(offsets):
        at = (depth_ref[0] + offset) % count
        block = grads[i][...]
        full_ref[at] = block
        for j in range(2):
            cols = pl.ds(pl.multiple_of((2 * j + 1 - core) * DH, DH), DH)
            send_ref[at, :, j * DH : (j + 1) * DH] = grads[i][:, cols]
        part = mm(block, weight_ref[:, pl.ds(pl.multiple_of(at * width, width), width)], ((1,), (1,)))
        total = part if total is None else total + part
    out_ref[...] = total.astype(BF16)


def slot_of(distance):
    return jnp.where(distance == 0, 0, jnp.where(distance == 3, 1, distance + 1))


def weight_term_kernel(place_ref, full_ref, other_grads, mine, other, *refs):
    outs, turned_ref, slots = refs[:4], refs[4], refs[5:]
    place = place_ref[0]
    core = place & 1
    rows, width = mine.shape
    part = width // 2
    turned_ref[:, :rows] = mine[...].astype(F32).T.astype(BF16)
    turned_ref[:, rows:] = other[...].astype(F32).T.astype(BF16)

    def term_of(at, carry):
        own = [full_ref[at, :, pl.ds(pl.multiple_of((2 * j + core) * DH, DH), DH)] for j in range(2)]
        own = jnp.concatenate(own, axis=1)
        term = mm(turned_ref[:, :rows], own, ((1,), (0,))) + mm(turned_ref[:, rows:], other_grads[at], ((1,), (0,)))
        term = term.astype(BF16)
        for j in range(2):
            chip = 2 * at + j
            slot_x = slot_of((chip >> 2) ^ (place >> 3))
            slot_y = slot_of((chip & 3) ^ ((place >> 1) & 3))
            slots[0][4 * slot_x + slot_y] = term[:part, j * DH : (j + 1) * DH]
            slots[1][4 * slot_y + slot_x] = term[part:, j * DH : (j + 1) * DH]
        return carry

    lax.fori_loop(0, full_ref.shape[0], term_of, 0)
    half = slots[0].shape[0] // 2
    for i in range(2):
        outs[2 * i][...] = slots[i][half:]
        outs[2 * i + 1][...] = slots[i][:half]


def column_weights(block_doc, my_block, leaf_rows, level_count):
    leaf_iota = jnp.arange(leaf_rows, dtype=jnp.int32)
    block_parts = [
        jnp.full((leaf_rows,), my_block, jnp.int32),
        jnp.full((leaf_rows,), my_block ^ 1, jnp.int32),
    ]
    weight_parts = [jnp.ones((2 * leaf_rows,), F32)]
    for level_num in range(1, level_count):
        group_first = (my_block >> level_num ^ 1) << level_num
        block_parts.append(group_first + leaf_iota // (leaf_rows >> level_num))
        weight_parts.append(jnp.full((leaf_rows,), 2.0**level_num, F32))
    col_block = jnp.concatenate(block_parts)
    col_weight = jnp.concatenate(weight_parts)
    block_ids = jnp.arange(block_doc.shape[1], dtype=jnp.int32)
    col_onehot = (block_ids[:, None] == col_block[None, :]).astype(jnp.int32)
    col_doc = jnp.sum(block_doc[0][:, None] * col_onehot, axis=0)
    own_doc = jnp.sum(block_doc[0] * (block_ids == my_block).astype(jnp.int32))
    return jnp.where(col_doc == own_doc, col_weight, 0.0)[None]


class RingGather:
    def __init__(self, block, axis):
        self.axis, self.count = axis, lax.axis_size(axis)
        self.below, self.above, self.steps = block, block, 0
        self.blocks = [(0, block)]

    def step(self, after):
        count, self.steps = self.count, self.steps + 1
        self.below, self.above, _ = lax.optimization_barrier((self.below, self.above, after))
        self.below = lax.ppermute(self.below, self.axis, [(i, (i + 1) % count) for i in range(count)])
        self.blocks.append((-self.steps % count, self.below))
        if self.steps < count - self.steps:
            self.above = lax.ppermute(self.above, self.axis, [(i, (i - 1) % count) for i in range(count)])
            self.blocks.append((self.steps, self.above))


N_PARTS = 1


def local(queries, keys, values, out_weight, out_grad, block_doc):
    seq_count = lax.axis_size("seq")
    level_count = seq_count.bit_length() - 1
    n_up = level_count - 1
    my_block = lax.axis_index("seq")
    place = my_block.astype(jnp.int32)[None]
    depth = lax.axis_index("head").astype(jnp.int32)[None]
    _, rows, features = queries.shape
    heads = features // DH
    part_heads = heads // N_PARTS
    part_width = part_heads * DH
    cols = (level_count + 1) * rows
    scaling = 1.0 / math.sqrt(DH)
    queries, keys, values = queries[0], keys[0], values[0]
    tall = (rows, part_width)

    other_keys = swapped(keys, 0)
    other_values = swapped(values, 0)
    ring = RingGather(out_grad[0], "head")
    ring.step(other_values)
    chains = list(
        near_call(
            pool_first_kernel,
            place,
            (other_keys, other_values),
            (keys, values),
            [(tall, BF16, True)] * N_PARTS,
            name="pool_leaf",
        )
    )
    mine, other = [[] for _ in chains], [[] for _ in chains]
    for level_num in range(1, level_count):
        for i in range(N_PARTS):
            got = swapped(chains[i], level_num)
            mine[i].append(got)
            other[i].append(swapped(got, 0))
            if level_num + 1 < level_count:
                (chains[i],) = near_call(
                    functools.partial(pool_kernel, level_num),
                    place,
                    (chains[i], got),
                    (),
                    [(tall, BF16, True)],
                    name="pool_group",
                )
        if level_num + 1 < level_count:
            ring.step(chains[0])
    offsets = tuple(o for o, _ in ring.blocks)
    full_grad = [b for _, b in ring.blocks]
    col_weight = column_weights(block_doc, my_block, rows, level_count)
    slab = pl.BlockSpec((rows, DH), lambda h: (0, h))
    col_slab = pl.BlockSpec((cols, DH), lambda h: (0, h))
    prob_slab = pl.BlockSpec((1, rows, cols), lambda h: (h, 0, 0))
    up_slab = pl.BlockSpec((n_up, rows, DH), lambda h: (0, 0, h))
    whole_slabs = [
        pl.BlockSpec((rows, DH), functools.partial(lambda first, h: (0, first + h), i * part_heads))
        for i in range(N_PARTS)
    ]
    forward = []
    for i in range(N_PARTS):
        forward.append(
            pl.pallas_call(
                functools.partial(forward_kernel, scaling, n_up),
                grid=(part_heads,),
                in_specs=[SMEM, pl.BlockSpec((1, cols), lambda h: (0, 0))]
                + [whole_slabs[i]] * 5
                + [slab] * (2 * n_up),
                out_specs=[slab, prob_slab, col_slab, col_slab],
                out_shape=[
                    jax.ShapeDtypeStruct(tall, BF16),
                    jax.ShapeDtypeStruct((part_heads, rows, cols), BF16),
                    jax.ShapeDtypeStruct((cols, part_width), BF16),
                    jax.ShapeDtypeStruct((cols, part_width), BF16),
                ],
                name="attention_forward",
            )(place, col_weight, queries, keys, other_keys, values, other_values, *mine[i], *other[i])
        )
    contexts = [f[0] for f in forward]
    out_weight = after(out_weight, contexts[0])
    context_grad, send_grad, stacked_grad = pl.pallas_call(
        functools.partial(context_grad_kernel, offsets),
        in_specs=[SMEM, SMEM] + [VMEM] * (1 + len(offsets)),
        out_specs=[VMEM, VMEM, VMEM],
        out_shape=[
            jax.ShapeDtypeStruct((rows, features), BF16),
            jax.ShapeDtypeStruct((len(offsets), rows, features // 2), BF16),
            jax.ShapeDtypeStruct((len(offsets), rows, features), BF16),
        ],
        name="context_grad",
    )(place, depth, out_weight, *full_grad)
    other_grad = swapped(send_grad, 0)

    partial_grads = []
    for i in range(N_PARTS):
        context, prob, kcols, vcols = forward[i]
        partial_grads.append(
            pl.pallas_call(
                functools.partial(backward_kernel, scaling, n_up),
                grid=(part_heads,),
                in_specs=[SMEM, whole_slabs[i], prob_slab, slab, whole_slabs[i], col_slab, col_slab],
                out_specs=[slab] * 5 + [up_slab, up_slab],
                out_shape=[jax.ShapeDtypeStruct(tall, BF16)]
                + [jax.ShapeDtypeStruct(tall, BF16)] * 4
                + [
                    jax.ShapeDtypeStruct((n_up,) + tall, BF16),
                    jax.ShapeDtypeStruct((n_up,) + tall, BF16),
                ],
                name="attention_backward",
            )(place, queries, prob, context, context_grad, kcols, vcols)
        )
    query_grad = jnp.concatenate([g[0] for g in partial_grads], axis=1)
    halves = [pltpu.VMEM(tall, BF16), pltpu.VMEM(tall, BF16)]
    keep = [g[5] for g in partial_grads]
    recv_up = [swapped(g[6], 0) for g in partial_grads]
    back, held, rest = [None] * N_PARTS, [None] * N_PARTS, [None] * N_PARTS
    for i in range(N_PARTS):
        send, *rest[i] = near_call(
            top_kernel,
            place,
            (recv_up[i],),
            (keep[i],),
            [(tall, BF16, True)] + [(tall, BF16, False)] * (n_up - 1),
            name="hand_down_top",
        )
        back[i] = swapped(send, level_count - 1)
    (context,) = contexts
    shape = (seq_count // 4, features // 2, DH)
    weight_outs = pl.pallas_call(
        weight_term_kernel,
        in_specs=[SMEM] + [VMEM] * 4,
        out_specs=[VMEM] * 4,
        out_shape=[jax.ShapeDtypeStruct(shape, BF16)] * 4,
        scratch_shapes=[pltpu.VMEM((features, 2 * rows), BF16)]
        + [pltpu.VMEM((seq_count // 2, features // 2, DH), BF16)] * 2,
        name="weight_term",
    )(place, after(stacked_grad, send), other_grad, context, swapped(context, 0))
    weight_parts = [
        HalvedSum(weight_outs[0], weight_outs[1], (3, 4, 1, 2)),
        HalvedSum(weight_outs[2], weight_outs[3], (1, 2, 3, 4)),
    ]
    for level_num in range(level_count - 2, 0, -1):
        if level_num < level_count - 2:
            for w in weight_parts:
                w.step()
        for i in range(N_PARTS):
            if level_num < level_count - 2:
                back[i] = after(back[i], *[w.send for w in weight_parts])
            send, held[i] = near_call(
                functools.partial(climb_kernel, level_num),
                place,
                (back[i],),
                (rest[i][level_num - 1],) + (() if held[i] is None else (held[i],)),
                [(tall, BF16, True), (tall, F32, False)],
                scratch=halves,
                name="hand_down",
            )
            back[i] = swapped(send, level_num)
    for w in weight_parts:
        w.step()
    back[-1] = after(back[-1], *[w.send for w in weight_parts])
    for w in weight_parts:
        w.step()
    weight_grad = jnp.concatenate([w.keep for w in weight_parts], axis=0)
    key_grads, value_grads = [], []
    for i in range(N_PARTS):
        send_k, send_v, total_k, total_v = near_call(
            leaf_kernel,
            place,
            (back[i],),
            (held[i],) + tuple(partial_grads[i][1:5]),
            [(tall, BF16, True), (tall, BF16, True), (tall, F32, True), (tall, F32, True)],
            scratch=halves,
            name="hand_down_leaf",
        )
        key_grads.append((total_k + swapped(send_k, 0).astype(F32)).astype(BF16))
        value_grads.append((total_v + swapped(send_v, 0).astype(F32)).astype(BF16))
    context = jnp.concatenate(contexts, axis=1)
    key_grad = jnp.concatenate(key_grads, axis=1)
    value_grad = jnp.concatenate(value_grads, axis=1)
    return context[None], query_grad[None], key_grad[None], value_grad[None], weight_grad


def after(value, *others):
    return lax.optimization_barrier((value,) + others)[0]


class HalvedSum:
    def __init__(self, send, keep, level_nums):
        self.send, self.keep, self.levels = send, keep, list(level_nums)

    def step(self):
        got = swapped(self.send, self.levels.pop(0))
        half = self.keep.shape[0] // 2
        if not self.levels:
            self.keep = (self.keep[0].astype(F32) + got[0].astype(F32)).astype(BF16)
            return
        self.send = (self.keep[half:].astype(F32) + got[half:].astype(F32)).astype(BF16)
        self.keep = self.keep[:half].astype(F32) + got[:half].astype(F32)


def solution(mesh):
    placed = (
        P(None, "seq", "head"),
        P(None, "seq", "head"),
        P(None, "seq", "head"),
        P("head", None),
        P(None, "seq", "head"),
        P(),
    )
    return jax.shard_map(
        local,
        mesh=mesh,
        in_specs=placed,
        out_specs=(
            P(None, "seq", "head"),
            P(None, "seq", "head"),
            P(None, "seq", "head"),
            P(None, "seq", "head"),
            P("head", "seq"),
        ),
        check_vma=False,
    )
```
